256 devices in a mesh: row: 16 (over x, y_lo, core), col: 16 (over y_hi, z).
Axes of the slice: x: 4, y: 4 (y_hi: 2, y_lo: 2; y = y_hi * 2 + y_lo), z: 8, core: 2. Of those that a mesh axis runs over, the one named last changes fastest.
Arguments:
- forcing_right_hand: float32 [4, 256, 2048], P(None, 'row', 'col'), may hold values from 0 to 2
- material: int32 [4, 256, 2048], P(None, 'row', 'col'), may hold values from 0 to 7
- capacity: float32 [8], replicated, may hold values from 0.3 to 3
- conductivity: float32 [8], replicated, may hold values from 0.2 to 2
- vent_open: float32 [256, 2048], P('row', 'col'), may hold values from 0.5 to 2
- partners: int32 [16, 16, 2], P('row', 'col'), may hold values from 0 to 15, as said below
- subspace_basis: bfloat16 [64, 4, 256, 2048], P(None, None, 'row', 'col'), may hold values from -0.5 to 1.5
Outputs:
- thermal_iterate: float32 [4, 256, 2048], P(None, 'row', 'col')
- defect_vector: float32 [4, 256, 2048], P(None, 'row', 'col')
- restricted_operator_blocks: float32 [16, 16, 16, 64, 64], P('row', 'col')
The draws below stay inside these ranges and needn't reach their ends.
Inputs may be any that keep to these rules, and one draw needn't show every extreme that they name: In each round the row indices of one col index pair up: partners[q, c, k] = r whenever partners[r, c, k] = q, and q never equals r.
All inputs are finite; a program needn't handle non-finite values.
Results may differ from the reference program's by a relative error of at most 0.01.
Values may be sent and summed in bfloat16 or wider, within the bound.
A program may use at most 64 MiB of HBM per device.

```python
import math
import jax
import jax.numpy as jnp
from jax import lax

GRID_WIDTH_EAST = 16
GRID_DEPTH_NORTH = 128
FLOOR_STRATA = 4
DEFL = 64
NCLASS = 8
NPAIR = 2
ITERS = 2
COARSE = 2
NX = 256
NY = 2048
N_ROW = 16
N_COL = 16


def draw_partners(key, part):
    round_keys = jax.random.split(key, N_COL * NPAIR)

    def one_round(round_key):
        shuffled = jax.random.permutation(round_key, N_ROW).astype(jnp.int32)
        inverse = jnp.argsort(shuffled, stable=True).astype(jnp.int32)
        position = inverse + 1 - 2 * (inverse % 2)
        return shuffled[position]
    rounds = jax.vmap(one_round)(round_keys)
    return rounds.reshape(N_COL, NPAIR, N_ROW).transpose(2, 0, 1).astype(jnp.int32)


def set_ends(array, rng, smallest, high):
    place = [jax.random.randint(jax.random.fold_in(rng, axis), (), 0, length) for axis, length in enumerate(array.shape)]
    widest = array.shape.index(max(array.shape))
    beside = place[:widest] + [(place[widest] + 1) % array.shape[widest]] + place[widest + 1:]
    return array.at[tuple(place)].set(smallest).at[tuple(beside)].set(high)


def shard_levels(stream_key, shape, cuts, low, largest):
    factor_of, own = 1.0, jax.random.fold_in(stream_key, 6)
    for dim, shards_of in cuts:
        steps = jnp.exp(jax.random.uniform(jax.random.fold_in(own, dim), (shards_of,), jnp.float32, low / len(cuts), largest / len(cuts)))
        factor_of = factor_of * jnp.repeat(steps, shape[dim] // shards_of).reshape([-1 if axis == dim else 1 for axis in range(len(shape))])
    return factor_of


def setup_inputs(seed: int = 0) -> dict:
    streams_of = jax.random.split(jax.random.key(seed), 8)
    return {
        "forcing_right_hand": jnp.clip(2.0 * jax.random.uniform(streams_of[0], (FLOOR_STRATA, NX, NY), jnp.float32) ** shard_levels(streams_of[0], (FLOOR_STRATA, NX, NY), ((1, 16), (2, 16)), -0.2, 0.2), 0.0, 2.0),
        "material": set_ends(jax.random.randint(streams_of[1], (FLOOR_STRATA, NX, NY), 0, NCLASS), jax.random.fold_in(streams_of[1], 1), 0, NCLASS - 1).astype(jnp.int32),
        "capacity": jnp.clip(jnp.exp(jax.random.uniform(streams_of[2], (NCLASS,), jnp.float32, math.log(0.3), math.log(3.0))), 0.3, 3.0),
        "conductivity": jnp.clip(jnp.exp(jax.random.uniform(streams_of[3], (NCLASS,), jnp.float32, math.log(0.2), math.log(2.0))), 0.2, 2.0),
        "vent_open": jnp.clip(jnp.exp(math.log(2.0) - 1.3862944 * jax.random.uniform(streams_of[4], (NX, NY), jnp.float32) ** shard_levels(streams_of[4], (NX, NY), ((0, 16), (1, 16)), -0.2, 0.2)), 0.5, 2.0),
        "partners": draw_partners(jax.random.fold_in(streams_of[7], 71), 0),
        "subspace_basis": jnp.clip(-0.5 + 2.0 * jax.random.uniform(streams_of[6], (DEFL, FLOOR_STRATA, NX, NY), jnp.float32) ** shard_levels(streams_of[6], (DEFL, FLOOR_STRATA, NX, NY), ((2, 16), (3, 16)), -0.2, 0.2), -0.5, 1.5).astype(jnp.bfloat16),
    }


highest = lax.Precision.HIGHEST
plenum_gain = 1.0

def harmonic(left_side, right_side):
    return 2.0 * left_side * right_side / (left_side + right_side)

def partner_sum(values, partners):
    blocks = values.reshape(N_ROW, GRID_WIDTH_EAST, N_COL, GRID_DEPTH_NORTH).transpose(0, 2, 1, 3)
    columns = jnp.arange(N_COL, dtype=jnp.int32)[None, :]
    global_accumulate = jnp.zeros(blocks.shape, jnp.float32)
    for pair_round in range(NPAIR):
        global_accumulate = global_accumulate + blocks[partners[:, :, pair_round], columns]
    return global_accumulate.transpose(0, 2, 1, 3).reshape(N_ROW * GRID_WIDTH_EAST, N_COL * GRID_DEPTH_NORTH)

def coefficients(material, capacity, conductivity, vent_open, partners):
    conduct_field = jnp.take(conductivity, material)
    capacity_field = jnp.take(capacity, material)
    padded = jnp.pad(conduct_field, 1)
    upper_z = harmonic(conduct_field, padded[2:, 1:-1, 1:-1])
    lower_z = harmonic(conduct_field, padded[:-2, 1:-1, 1:-1])
    upper_x = harmonic(conduct_field, padded[1:-1, 2:, 1:-1])
    lower_x = harmonic(conduct_field, padded[1:-1, :-2, 1:-1])
    upper_y = harmonic(conduct_field, padded[1:-1, 1:-1, 2:])
    lower_y = harmonic(conduct_field, padded[1:-1, 1:-1, :-2])
    diagonal = capacity_field + upper_z + lower_z + upper_x + lower_x + upper_y + lower_y
    vent_sum = partner_sum(vent_open, partners)
    diagonal = diagonal.at[FLOOR_STRATA - 1].add(plenum_gain * vent_open * vent_sum)
    return (diagonal, upper_z, lower_z, upper_x, lower_x, upper_y, lower_y)

def operate(values, coef_parts, vent_open, partners):
    diagonal, upper_z, lower_z, upper_x, lower_x, upper_y, lower_y = coef_parts
    padded = jnp.pad(values, 1)
    beside_all = upper_z * padded[2:, 1:-1, 1:-1] + lower_z * padded[:-2, 1:-1, 1:-1]
    beside_all = beside_all + upper_x * padded[1:-1, 2:, 1:-1] + lower_x * padded[1:-1, :-2, 1:-1]
    beside_all = beside_all + upper_y * padded[1:-1, 1:-1, 2:] + lower_y * padded[1:-1, 1:-1, :-2]
    result = diagonal * values - beside_all
    coupled = partner_sum(vent_open * values[FLOOR_STRATA - 1], partners)
    return result.at[FLOOR_STRATA - 1].add(-plenum_gain * vent_open * coupled)

def local_apply(basis_block, coef_parts):
    diagonal, upper_z, lower_z, upper_x, lower_x, upper_y, lower_y = coef_parts
    padded = jnp.pad(basis_block, ((0, 0), (1, 1), (1, 1), (1, 1)))
    beside_all = upper_z * padded[:, 2:, 1:-1, 1:-1] + lower_z * padded[:, :-2, 1:-1, 1:-1]
    beside_all = beside_all + upper_x * padded[:, 1:-1, 2:, 1:-1] + lower_x * padded[:, 1:-1, :-2, 1:-1]
    beside_all = beside_all + upper_y * padded[:, 1:-1, 1:-1, 2:] + lower_y * padded[:, 1:-1, 1:-1, :-2]
    return diagonal * basis_block - beside_all

def galerkin_blocks(subspace_basis, coef_parts, vent_open, partners):
    upper_x = coef_parts[3]
    upper_y = coef_parts[5]
    rows_index = jnp.repeat(jnp.arange(N_ROW, dtype=jnp.int32), N_COL)
    cols_index = jnp.tile(jnp.arange(N_COL, dtype=jnp.int32), N_ROW)

    def own_block(position):
        start_x = position[0] * GRID_WIDTH_EAST
        start_y = position[1] * GRID_DEPTH_NORTH
        anchor = jnp.zeros((), jnp.int32)
        basis_block = lax.dynamic_slice(subspace_basis, (anchor, anchor, start_x, start_y), (DEFL, FLOOR_STRATA, GRID_WIDTH_EAST, GRID_DEPTH_NORTH)).astype(jnp.float32)
        block_parts = [lax.dynamic_slice(coef_part, (anchor, start_x, start_y), (FLOOR_STRATA, GRID_WIDTH_EAST, GRID_DEPTH_NORTH)) for coef_part in coef_parts]
        applied = local_apply(basis_block, block_parts)
        return jnp.dot(basis_block.reshape(DEFL, -1), applied.reshape(DEFL, -1).T, precision=highest)
    diagonal = lax.map(own_block, jnp.stack([rows_index, cols_index], axis=1)).reshape(N_ROW, N_COL, DEFL, DEFL)
    last_x = subspace_basis[:, :, GRID_WIDTH_EAST - 1::GRID_WIDTH_EAST, :].astype(jnp.float32)
    first_x = subspace_basis[:, :, 0::GRID_WIDTH_EAST, :].astype(jnp.float32)
    next_x = jnp.concatenate([first_x[:, :, 1:], jnp.zeros_like(first_x[:, :, :1])], axis=2)
    weighted_x = (last_x * upper_x[:, GRID_WIDTH_EAST - 1::GRID_WIDTH_EAST, :]).reshape(DEFL, FLOOR_STRATA, N_ROW, N_COL, GRID_DEPTH_NORTH)
    ahead_x = -jnp.einsum('azrcy,bzrcy->rcab', weighted_x, next_x.reshape(DEFL, FLOOR_STRATA, N_ROW, N_COL, GRID_DEPTH_NORTH), precision=highest)
    behind_x = jnp.concatenate([jnp.zeros_like(ahead_x[:1]), ahead_x[:-1]], axis=0).transpose(0, 1, 3, 2)
    last_y = subspace_basis[:, :, :, GRID_DEPTH_NORTH - 1::GRID_DEPTH_NORTH].astype(jnp.float32)
    first_y = subspace_basis[:, :, :, 0::GRID_DEPTH_NORTH].astype(jnp.float32)
    next_y = jnp.concatenate([first_y[:, :, :, 1:], jnp.zeros_like(first_y[:, :, :, :1])], axis=3)
    weighted_y = (last_y * upper_y[:, :, GRID_DEPTH_NORTH - 1::GRID_DEPTH_NORTH]).reshape(DEFL, FLOOR_STRATA, N_ROW, GRID_WIDTH_EAST, N_COL)
    upper_col = -jnp.einsum('azrxc,bzrxc->rcab', weighted_y, next_y.reshape(DEFL, FLOOR_STRATA, N_ROW, GRID_WIDTH_EAST, N_COL), precision=highest)
    lower_col = jnp.concatenate([jnp.zeros_like(upper_col[:, :1]), upper_col[:, :-1]], axis=1).transpose(0, 1, 3, 2)
    row_numbers = jnp.arange(N_ROW, dtype=jnp.int32)
    row_grid = row_numbers[:, None, None]
    own_hot = (row_grid == row_numbers).astype(jnp.float32)
    next_hot = (row_grid + 1 == row_numbers).astype(jnp.float32)
    prev_hot = (row_grid - 1 == row_numbers).astype(jnp.float32)
    global_accumulate = diagonal[:, :, None] * own_hot[..., None, None] + ahead_x[:, :, None] * next_hot[..., None, None]
    global_accumulate = global_accumulate + behind_x[:, :, None] * prev_hot[..., None, None]
    top_layer = subspace_basis[:, FLOOR_STRATA - 1].astype(jnp.float32) * vent_open
    top_blocks = top_layer.reshape(DEFL, N_ROW, GRID_WIDTH_EAST, N_COL, GRID_DEPTH_NORTH).transpose(1, 3, 0, 2, 4).reshape(N_ROW, N_COL, DEFL, GRID_WIDTH_EAST * GRID_DEPTH_NORTH)
    columns = jnp.arange(N_COL, dtype=jnp.int32)[None, :]
    for pair_round in range(NPAIR):
        target = partners[:, :, pair_round]
        partner_top = top_blocks[target, columns]
        coupled = -plenum_gain * jnp.einsum('rcas,rcbs->rcab', top_blocks, partner_top, precision=highest)
        target_hot = (target[:, :, None] == row_numbers).astype(jnp.float32)
        global_accumulate = global_accumulate + target_hot[..., None, None] * coupled[:, :, None]
    return (global_accumulate, diagonal, lower_col, upper_col)

def remove_subspace_part(subspace_basis, values):

    def one_row(row_number):
        basis_row = lax.dynamic_slice_in_dim(subspace_basis, row_number * GRID_WIDTH_EAST, GRID_WIDTH_EAST, 2).astype(jnp.float32)
        values_row = lax.dynamic_slice_in_dim(values, row_number * GRID_WIDTH_EAST, GRID_WIDTH_EAST, 1)
        return jnp.einsum('azxcy,zxcy->ca', basis_row.reshape(DEFL, FLOOR_STRATA, GRID_WIDTH_EAST, N_COL, GRID_DEPTH_NORTH), values_row.reshape(FLOOR_STRATA, GRID_WIDTH_EAST, N_COL, GRID_DEPTH_NORTH), precision=highest)
    return lax.map(one_row, jnp.arange(N_ROW, dtype=jnp.int32))

def extend_subspace_values(subspace_basis, coarse_vector):

    def one_row(row_number):
        basis_row = lax.dynamic_slice_in_dim(subspace_basis, row_number * GRID_WIDTH_EAST, GRID_WIDTH_EAST, 2).astype(jnp.float32)
        spread_subspace_values = jnp.einsum('azxcy,ca->zxcy', basis_row.reshape(DEFL, FLOOR_STRATA, GRID_WIDTH_EAST, N_COL, GRID_DEPTH_NORTH), coarse_vector[row_number], precision=highest)
        return spread_subspace_values.reshape(FLOOR_STRATA, GRID_WIDTH_EAST, N_COL * GRID_DEPTH_NORTH)
    stacked = lax.map(one_row, jnp.arange(N_ROW, dtype=jnp.int32))
    return stacked.transpose(1, 0, 2, 3).reshape(FLOOR_STRATA, N_ROW * GRID_WIDTH_EAST, N_COL * GRID_DEPTH_NORTH)

def solve_one(factor, right_side):
    return jax.scipy.linalg.cho_solve((factor, True), right_side)

def reference(forcing_right_hand, material, capacity, conductivity, vent_open, partners, subspace_basis):
    coef_parts = coefficients(material, capacity, conductivity, vent_open, partners)
    global_accumulate, diagonal, lower_col, upper_col = galerkin_blocks(subspace_basis, coef_parts, vent_open, partners)
    factors = jnp.linalg.cholesky(diagonal)
    solve_all = jax.vmap(jax.vmap(solve_one))

    def coarse_apply(values):
        along = jnp.einsum('rcqab,qcb->rca', global_accumulate, values, precision=highest)
        before = jnp.concatenate([jnp.zeros_like(values[:, :1]), values[:, :-1]], axis=1)
        after = jnp.concatenate([values[:, 1:], jnp.zeros_like(values[:, :1])], axis=1)
        along = along + jnp.einsum('rcab,rcb->rca', lower_col, before, precision=highest)
        return along + jnp.einsum('rcab,rcb->rca', upper_col, after, precision=highest)

    def invert_galerkin_operator(right_side):
        values = solve_all(factors, right_side)
        for sweep_count in range(COARSE - 1):
            values = values + solve_all(factors, right_side - coarse_apply(values))
        return values

    def operator_apply(values):
        return operate(values, coef_parts, vent_open, partners)
    thermal_iterate = extend_subspace_values(subspace_basis, invert_galerkin_operator(remove_subspace_part(subspace_basis, forcing_right_hand)))
    defect_vector = forcing_right_hand - operator_apply(thermal_iterate)
    conjugate_update = defect_vector - extend_subspace_values(subspace_basis, invert_galerkin_operator(remove_subspace_part(subspace_basis, operator_apply(defect_vector))))
    norm_now = jnp.sum(defect_vector * defect_vector)
    for iteration in range(ITERS):
        applied = operator_apply(conjugate_update)
        update_factor = norm_now / jnp.sum(conjugate_update * applied)
        thermal_iterate = thermal_iterate + update_factor * conjugate_update
        defect_vector = defect_vector - update_factor * applied
        if iteration + 1 < ITERS:
            norm_next = jnp.sum(defect_vector * defect_vector)
            correction = extend_subspace_values(subspace_basis, invert_galerkin_operator(remove_subspace_part(subspace_basis, operator_apply(defect_vector))))
            conjugate_update = norm_next / norm_now * conjugate_update + defect_vector - correction
            norm_now = norm_next
    return (thermal_iterate, defect_vector, global_accumulate / (FLOOR_STRATA * GRID_WIDTH_EAST * GRID_DEPTH_NORTH))
```

```python
import functools

import jax
import jax.numpy as jnp
from jax import lax
from jax.experimental import pallas as pl
from jax.experimental.pallas import tpu as pltpu
from jax.sharding import PartitionSpec as P

MESH = pl.DeviceIdType.MESH
F32, BF16 = jnp.float32, jnp.bfloat16
LANES = 128
PIVOTS = 4
ROUNDS = 9


def harmonic(left_side, right_side):
    return 2.0 * left_side * right_side / (left_side + right_side)


def split(values):
    high = values.astype(BF16)
    return high, (values - high.astype(F32)).astype(BF16)


def dot_t(left, right):
    return lax.dot_general(left, right, (((1,), (1,)), ((), ())), preferred_element_type=F32)


def inverse(matrix):
    n = matrix.shape[0]
    row_id = lax.broadcasted_iota(jnp.int32, (n, n), 0)
    col_id = lax.broadcasted_iota(jnp.int32, (n, n), 1)
    work = jnp.concatenate([matrix, (row_id == col_id).astype(F32)], axis=1)
    wide_row = lax.broadcasted_iota(jnp.int32, work.shape, 0)
    for base in range(0, n, PIVOTS):
        ids = range(PIVOTS)
        rows = [work[base + i : base + i + 1, :] for i in ids]
        pivot = [
            [jnp.broadcast_to(rows[i][:, base + j : base + j + 1], rows[i].shape) for j in ids]
            for i in ids
        ]
        inside = (wide_row >= base) & (wide_row < base + PIVOTS)
        columns = [
            jnp.where(
                inside,
                jnp.where(wide_row == base + j, -1.0, 0.0),
                jnp.broadcast_to(work[:, base + j : base + j + 1], work.shape),
            )
            for j in ids
        ]
        work = jnp.where(inside, 0.0, work)
        for p in ids:
            scale = 1.0 / pivot[p][p]
            rows[p] = rows[p] * scale
            for j in range(p + 1, PIVOTS):
                pivot[p][j] = pivot[p][j] * scale
            for i in ids:
                if i != p:
                    factor = pivot[i][p]
                    rows[i] = rows[i] - factor * rows[p]
                    for j in range(p + 1, PIVOTS):
                        pivot[i][j] = pivot[i][j] - factor * pivot[p][j]
        for j in ids:
            work = work - columns[j] * rows[j]
    return work[:, n:]


def kernel(
    n_row, n_col,
    cap_ref, con_ref, par_ref, rhs_ref, mat_ref, vent_ref, basis_ref,
    x_ref, r_ref, e_ref,
    fields, ysend, yrecv, info, zf, zk, zr, az, xb, pa, pb, pc, coef, work, wide, inv_ref,
    red_row, red_col,
    top_s, top_r, x_s, x_r, y_s, y_r, info_s, info_r, xb_s, xb_r, pa_s, pa_r, pc_s, pc_r,
    rr_s, rr_r, rc_s, rc_r, *tops,
):
    layers, width, depth = rhs_ref.shape
    vectors = basis_ref.shape[0]
    lines = layers * width
    share = width // n_row
    row, col = lax.axis_index("row"), lax.axis_index("col")
    row_up, row_dn = lax.rem(row + 1, n_row), lax.rem(row + n_row - 1, n_row)
    col_up, col_dn = lax.rem(col + 1, n_col), lax.rem(col + n_col - 1, n_col)

    def peer(i, me, count):
        return lax.rem(me + i, count)

    def remote(src, dst, send, recv, target):
        return pltpu.make_async_remote_copy(
            src_ref=src, dst_ref=dst, send_sem=send, recv_sem=recv,
            device_id=target, device_id_type=MESH,
        )

    def wait_bytes(ref, sem):
        pltpu.make_async_copy(ref, ref, sem).wait()

    barrier = pltpu.get_barrier_semaphore()

    @pl.loop(1, n_row)
    def _(i):
        pl.semaphore_signal(
            barrier, inc=1, device_id=(peer(i, row, n_row), col), device_id_type=MESH
        )

    @pl.loop(1, n_col)
    def _(i):
        pl.semaphore_signal(
            barrier, inc=1, device_id=(row, peer(i, col, n_col)), device_id_type=MESH
        )

    material = mat_ref[...]
    conduct = jnp.zeros(material.shape, F32)
    heat = jnp.zeros(material.shape, F32)
    for class_id in range(con_ref.shape[0]):
        hit = material == class_id
        conduct = jnp.where(hit, con_ref[class_id], conduct)
        heat = jnp.where(hit, cap_ref[class_id], heat)
    vent = vent_ref[...]
    partner = [par_ref[k] for k in range(2)]
    info_row = lax.broadcasted_iota(jnp.int32, (8, LANES), 0)
    info[row] = jnp.where(
        info_row == 0, partner[0].astype(F32), jnp.where(info_row == 1, partner[1].astype(F32), 0.0)
    )
    lane = lax.broadcasted_iota(jnp.int32, (8, LANES), 1)
    groups = lines // 8

    def start_exchange(at, values, top):
        fields[at, :, 8 : 8 + width, :] = values
        tops[at][row] = top
        tiles = values.reshape(groups, 8, depth)
        packed = jnp.zeros((8, LANES), F32)
        for j in range(groups):
            packed = jnp.where(lane == j, pltpu.roll(tiles[j], j, 1), packed)
            packed = jnp.where(
                lane == groups + j, pltpu.roll(tiles[j], groups + j + 1, 1), packed
            )
        ysend[at] = packed

        @pl.loop(1, n_row)
        def _(i):
            remote(
                tops[at].at[row], tops[at].at[row], top_s.at[at], top_r.at[at],
                (peer(i, row, n_row), col),
            ).start()

        for copy in side_copies(at):
            copy.start()

    def side_copies(at):
        return (
            remote(
                fields.at[at, :, pl.ds(7 + width, 1), :], fields.at[at, :, pl.ds(7, 1), :],
                x_s.at[at, 0], x_r.at[at, 0], (row_up, col),
            ),
            remote(
                fields.at[at, :, pl.ds(8, 1), :], fields.at[at, :, pl.ds(8 + width, 1), :],
                x_s.at[at, 1], x_r.at[at, 1], (row_dn, col),
            ),
            remote(ysend.at[at], yrecv.at[at, 0], y_s.at[at, 0], y_r.at[at, 0], (row, col_up)),
            remote(ysend.at[at], yrecv.at[at, 1], y_s.at[at, 1], y_r.at[at, 1], (row, col_dn)),
        )

    def finish_exchange(at, values):
        for copy in side_copies(at):
            copy.wait_recv()
        wait_bytes(tops[at].at[pl.ds(0, n_row - 1)], top_r.at[at])
        tiles = values.reshape(groups, 8, depth)
        from_dn, from_up = yrecv[at, 0], yrecv[at, 1]
        dn_y, up_y = [], []
        for j in range(groups):
            dn_y.append(
                pltpu.roll(
                    jnp.where(
                        lane == LANES - 1, pltpu.roll(from_dn, LANES - 1 - groups - j, 1), tiles[j]
                    ),
                    1, 1,
                )
            )
            up_y.append(
                pltpu.roll(
                    jnp.where(lane == 0, pltpu.roll(from_up, (LANES - j) % LANES, 1), tiles[j]),
                    LANES - 1, 1,
                )
            )
        dn_y = jnp.stack(dn_y).reshape(values.shape)
        up_y = jnp.stack(up_y).reshape(values.shape)
        dn_x = fields[at, :, 7 : 7 + width, :]
        up_x = fields[at, :, 9 : 9 + width, :]
        coupled = tops[at][partner[0]] + tops[at][partner[1]]
        return up_x, dn_x, up_y, dn_y, coupled

    pl.semaphore_wait(barrier, n_row - 1 + n_col - 1)
    start_exchange(0, conduct, vent)

    @pl.loop(1, n_row)
    def _(i):
        remote(info.at[row], info.at[row], info_s, info_r, (peer(i, row, n_row), col)).start()

    @pl.loop(0, vectors)
    def _(a):
        zf[pl.ds(a * lines, lines), :] = basis_ref[a].astype(F32)

    pad = width * vectors
    zk[0:pad, :] = jnp.zeros((pad, depth), F32)
    zk[pad + lines * vectors :, :] = jnp.zeros((pad, depth), F32)

    def line(k):
        return pl.ds(pad + k * vectors, vectors)

    @pl.loop(0, lines)
    def _(k):
        block = zf[pl.ds(k, vectors, stride=lines), :]
        zk[line(k), :] = block
        zr[:, pl.ds(pl.multiple_of(k * depth, depth), depth)] = block.astype(BF16)

    def cells(k):
        return pl.ds(pl.multiple_of(k * depth, depth), depth)

    def face_copies():
        copies = []
        for z in range(layers):
            there = pl.ds(z * depth, depth)
            copies.append(
                remote(
                    zr.at[:, cells(z * width + width - 1)], xb.at[0, :, there],
                    xb_s.at[0, z], xb_r.at[0, z], (row_up, col),
                )
            )
            copies.append(
                remote(
                    zr.at[:, cells(z * width)], xb.at[1, :, there],
                    xb_s.at[1, z], xb_r.at[1, z], (row_dn, col),
                )
            )
        return copies

    top_line = (layers - 1) * width
    for copy in face_copies():
        copy.start()

    @pl.loop(1, n_row)
    def _(i):
        target = peer(i, row, n_row)
        first = top_line + target * share
        remote(
            zr.at[:, pl.ds(pl.multiple_of(first * depth, depth), share * depth)], pa.at[row],
            pa_s, pa_r, (target, col),
        ).start()

    def project(values):
        work[...] = values.reshape(lines, depth)

        def step(k, total):
            return total + zk[line(k), :] * work[pl.ds(k, 1), :]

        total = lax.fori_loop(0, lines, step, jnp.zeros((vectors, depth), F32), unroll=8)
        return jnp.sum(total, axis=1, keepdims=True)

    def expand(coarse):
        wide[...] = jnp.broadcast_to(coarse, wide.shape)

        def step(a, total):
            return total + zf[pl.ds(a * lines, lines), :] * wide[pl.ds(a, 1), :]

        total = lax.fori_loop(0, vectors, step, jnp.zeros((lines, depth), F32), unroll=8)
        return total.reshape(layers, width, depth)

    square_row = lax.broadcasted_iota(jnp.int32, (vectors, vectors), 0)
    square_col = lax.broadcasted_iota(jnp.int32, (vectors, vectors), 1)

    def solve(right_side):
        flat = jnp.sum(jnp.where(square_row == square_col, right_side, 0.0), axis=0, keepdims=True)
        return jnp.sum(inv_ref[...] * flat, axis=1, keepdims=True)

    rhs = rhs_ref[...]
    first_side = project(rhs)

    near = finish_exchange(0, conduct)
    none = jnp.zeros((1, width, depth), F32)
    up_z = jnp.concatenate([harmonic(conduct[:-1], conduct[1:]), none], axis=0)
    dn_z = jnp.concatenate([none, up_z[:-1]], axis=0)
    x_id = lax.broadcasted_iota(jnp.int32, conduct.shape, 1)
    y_id = lax.broadcasted_iota(jnp.int32, conduct.shape, 2)
    x_last, x_first = x_id == width - 1, x_id == 0
    y_last, y_first = y_id == depth - 1, y_id == 0
    up_x = jnp.where(x_last & (row == n_row - 1), 0.0, harmonic(conduct, near[0]))
    dn_x = jnp.where(x_first & (row == 0), 0.0, harmonic(conduct, near[1]))
    up_y = jnp.where(y_last & (col == n_col - 1), 0.0, harmonic(conduct, near[2]))
    dn_y = jnp.where(y_first & (col == 0), 0.0, harmonic(conduct, near[3]))
    diagonal = heat + up_z + dn_z + up_x + dn_x + up_y + dn_y
    diagonal = jnp.concatenate(
        [diagonal[:-1], (diagonal[-1] + vent * near[4])[None]], axis=0
    )

    local = (
        diagonal, up_z, dn_z,
        jnp.where(x_last, 0.0, up_x), jnp.where(x_first, 0.0, dn_x),
        jnp.where(y_last, 0.0, up_y), jnp.where(y_first, 0.0, dn_y),
    )
    for c in range(7):
        coef[c] = local[c].reshape(lines, depth)

    @pl.loop(0, lines)
    def _(k):
        own = zk[line(k), :]

        def at(c):
            return coef[c, pl.ds(k, 1), :]

        applied = at(0) * own
        applied = applied - at(1) * zk[line(k + width), :] - at(2) * zk[line(k - width), :]
        applied = applied - at(3) * zk[line(k + 1), :] - at(4) * zk[line(k - 1), :]
        applied = applied - at(5) * pltpu.roll(own, depth - 1, 1) - at(6) * pltpu.roll(own, 1, 1)
        high, low = split(applied)
        az[0:vectors, cells(k)] = high
        az[vectors : 2 * vectors, cells(k)] = low

    both = dot_t(az[...], zr[...])
    own_block = both[:vectors] + both[vectors:]
    inv_ref[...] = inverse(own_block)

    def apply_start(at, values):
        start_exchange(at, values, vent * values[layers - 1])

    def apply_finish(at, values):
        near = finish_exchange(at, values)
        none = jnp.zeros((1, width, depth), F32)
        result = diagonal * values
        result = result - up_z * jnp.concatenate([values[1:], none], axis=0)
        result = result - dn_z * jnp.concatenate([none, values[:-1]], axis=0)
        result = result - up_x * near[0] - dn_x * near[1] - up_y * near[2] - dn_y * near[3]
        return jnp.concatenate([result[:-1], (result[-1] - vent * near[4])[None]], axis=0)

    def apply(at, values, beside=None):
        apply_start(at, values)
        if beside is not None:
            beside()
        return apply_finish(at, values)

    def correct(at, right_side, besides):
        first = expand(solve(right_side))
        first_image = apply(at, first, besides[0])
        second = expand(solve(right_side - project(first_image)))
        second_image = apply(at + 1, second, besides[1])
        return first + second, first_image + second_image

    def faces():
        for copy in face_copies():
            copy.wait_recv()
        for side, at, coefficient in ((0, 0, dn_x), (1, width - 1, up_x)):
            terms = [
                zk[line(z * width + at), :] * coefficient[z, at : at + 1, :] for z in range(layers)
            ]
            high, low = split(jnp.concatenate(terms, axis=1))
            both = dot_t(jnp.concatenate([high, low], axis=0), xb[side])
            wide_faces[side] = both[:vectors] + both[vectors:]

    wide_faces = [None, None]

    def plenum():
        wait_bytes(info.at[pl.ds(0, n_row - 1)], info_r)
        wait_bytes(pa.at[pl.ds(0, n_row - 1)], pa_r)
        first = top_line + row * share
        pa[row] = zr[:, pl.ds(pl.multiple_of(first * depth, depth), share * depth)]

        @pl.loop(0, n_row)
        def _(s):
            own = pa[s]
            total = None
            for i in range(share):
                rows = []
                for k in range(2):
                    which = info[s, k : k + 1, :]
                    chosen = jnp.zeros((vectors, depth), F32)
                    gain = jnp.zeros((1, depth), F32)
                    for t in range(n_row):
                        block = pa[t, :, i * depth : (i + 1) * depth].astype(F32)
                        gain = jnp.where(which == t, tops[0][t, pl.ds(row * share + i, 1), :], gain)
                        chosen = jnp.where(which == t, block, chosen)
                    rows.append(chosen * (gain * tops[0][s, pl.ds(row * share + i, 1), :]))
                high, low = split(jnp.concatenate(rows, axis=0))
                mine = own[:, i * depth : (i + 1) * depth]
                part = dot_t(
                    jnp.concatenate([mine, mine], axis=1), jnp.concatenate([high, low], axis=1)
                )
                total = part if total is None else total + part
            pb[s] = total

        @pl.loop(1, n_row)
        def _(i):
            target = peer(i, row, n_row)
            remote(pb.at[target], pc.at[row], pc_s, pc_r, (target, col)).start()

        pc[row] = pb[row]

    def finish_blocks():
        wait_bytes(pc.at[pl.ds(0, n_row - 1)], pc_r)
        total = lax.fori_loop(
            0, n_row, lambda i, t: t + pc[i], jnp.zeros((vectors, 2 * vectors), F32)
        )
        scale = 1.0 / (lines * depth)
        parts = (
            own_block * scale, wide_faces[0] * -scale, wide_faces[1] * -scale,
            total[:, :vectors] * -scale, total[:, vectors:] * -scale,
        )

        @pl.loop(0, n_row)
        def _(q):
            hits = (q == row, q == row - 1, q == row + 1, q == partner[0], q == partner[1])
            value = jnp.zeros((vectors, vectors), F32)
            for hit, part in zip(hits, parts):
                value = value + jnp.where(hit, 1.0, 0.0) * part
            e_ref[q] = value

    iterate, image = correct(1, first_side, (faces, None))
    defect = rhs - image
    turned = apply(3, defect)
    shift, image = correct(4, project(turned), (plenum, None))
    direction, stepped = defect - shift, turned - image
    turned = apply(6, stepped)
    shift, image = correct(7, project(turned), (None, finish_blocks))
    slanted, slanted_image = stepped - shift, turned - image

    def lanes_of(left, right):
        return jnp.sum((left * right).reshape(lines, depth), axis=0, keepdims=True)

    sums = [
        lanes_of(defect, defect), lanes_of(direction, stepped), lanes_of(defect, stepped),
        lanes_of(stepped, stepped), lanes_of(slanted, stepped), lanes_of(slanted, slanted_image),
    ]
    red_row[row] = jnp.concatenate(sums + [jnp.zeros((2, depth), F32)], axis=0)

    @pl.loop(1, n_row)
    def _(i):
        remote(red_row.at[row], red_row.at[row], rr_s, rr_r, (peer(i, row, n_row), col)).start()

    wait_bytes(red_row.at[pl.ds(0, n_row - 1)], rr_r)
    red_col[col] = jnp.sum(red_row[...], axis=0)

    @pl.loop(1, n_col)
    def _(i):
        remote(red_col.at[col], red_col.at[col], rc_s, rc_r, (row, peer(i, col, n_col))).start()

    wait_bytes(red_col.at[pl.ds(0, n_col - 1)], rc_r)
    scalars = jnp.sum(jnp.sum(red_col[...], axis=0), axis=1, keepdims=True)
    norm, curve, cross, square, mixed, slant = [scalars[i : i + 1, :] for i in range(6)]
    alpha = norm / curve
    after = norm - 2.0 * alpha * cross + alpha * alpha * square
    more = 1.0 + after / norm
    curve = more * more * curve - 2.0 * more * alpha * mixed + alpha * alpha * slant
    last = after / curve

    def scaled(factor, values):
        return jnp.broadcast_to(factor, values.shape) * values

    alpha, more, last = alpha[None], more[None], last[None]
    x_ref[...] = (
        iterate
        + scaled(alpha, direction)
        + scaled(last, scaled(more, direction) - scaled(alpha, slanted))
    )
    r_ref[...] = (
        defect
        - scaled(alpha, stepped)
        - scaled(last, scaled(more, stepped) - scaled(alpha, slanted_image))
    )

    for at in range(ROUNDS):
        for copy in side_copies(at):
            copy.wait_send()
        wait_bytes(tops[at].at[pl.ds(0, n_row - 1)], top_s.at[at])

    for copy in face_copies():
        copy.wait_send()
    wait_bytes(info.at[pl.ds(0, n_row - 1)], info_s)
    wait_bytes(pa.at[pl.ds(0, n_row - 1)], pa_s)
    wait_bytes(pc.at[pl.ds(0, n_row - 1)], pc_s)
    wait_bytes(red_row.at[pl.ds(0, n_row - 1)], rr_s)
    wait_bytes(red_col.at[pl.ds(0, n_col - 1)], rc_s)


def body(n_row, n_col, rhs, material, capacity, conductivity, vent, partners, basis):
    layers, width, depth = rhs.shape
    vectors = basis.shape[0]
    lines, share = layers * width, width // n_row
    smem, vmem = pl.BlockSpec(memory_space=pltpu.SMEM), pl.BlockSpec(memory_space=pltpu.VMEM)
    dma = pltpu.SemaphoreType.DMA
    scratch = [
        pltpu.VMEM((ROUNDS, layers, width + 16, depth), F32),
        pltpu.VMEM((ROUNDS, 8, LANES), F32),
        pltpu.VMEM((ROUNDS, 2, 8, LANES), F32),
        pltpu.VMEM((n_row, 8, LANES), F32),
        pltpu.VMEM((vectors * lines, depth), F32),
        pltpu.VMEM((vectors * (lines + 2 * width), depth), F32),
        pltpu.VMEM((vectors, lines * depth), BF16),
        pltpu.VMEM((2 * vectors, lines * depth), BF16),
        pltpu.VMEM((2, vectors, layers * depth), BF16),
        pltpu.VMEM((n_row, vectors, share * depth), BF16),
        pltpu.VMEM((n_row, vectors, 2 * vectors), F32),
        pltpu.VMEM((n_row, vectors, 2 * vectors), F32),
        pltpu.VMEM((7, lines, depth), F32),
        pltpu.VMEM((lines, depth), F32),
        pltpu.VMEM((vectors, depth), F32),
        pltpu.VMEM((vectors, vectors), F32),
        pltpu.VMEM((n_row, 8, LANES), F32),
        pltpu.VMEM((n_col, 8, LANES), F32),
        dma((ROUNDS,)), dma((ROUNDS,)), dma((ROUNDS, 2)), dma((ROUNDS, 2)),
        dma((ROUNDS, 2)), dma((ROUNDS, 2)), dma, dma, dma((2, layers)), dma((2, layers)),
        dma, dma, dma, dma, dma, dma, dma, dma,
        *[pltpu.VMEM((n_row, width, depth), F32) for _ in range(ROUNDS)],
    ]
    iterate, defect, blocks = pl.pallas_call(
        functools.partial(kernel, n_row, n_col),
        out_shape=(
            jax.ShapeDtypeStruct(rhs.shape, F32),
            jax.ShapeDtypeStruct(rhs.shape, F32),
            jax.ShapeDtypeStruct((n_row, vectors, vectors), F32),
        ),
        in_specs=[smem, smem, smem, vmem, vmem, vmem, vmem],
        out_specs=(vmem, vmem, vmem),
        scratch_shapes=scratch,
        compiler_params=pltpu.CompilerParams(
            collective_id=0, has_side_effects=True, vmem_limit_bytes=48 * 1024 * 1024
        ),
        name="deflated_cg",
    )(
        capacity, conductivity, partners.reshape(-1), rhs, material, vent,
        basis.reshape(vectors, lines, depth),
    )
    return iterate, defect, blocks[None, None]


def solution(mesh):
    n_row, n_col = mesh.shape["row"], mesh.shape["col"]
    return jax.shard_map(
        functools.partial(body, n_row, n_col),
        mesh=mesh,
        in_specs=(
            P(None, "row", "col"),
            P(None, "row", "col"),
            P(),
            P(),
            P("row", "col"),
            P("row", "col", None),
            P(None, None, "row", "col"),
        ),
        out_specs=(P(None, "row", "col"), P(None, "row", "col"), P("row", "col", None, None, None)),
        check_vma=False,
    )
```

```python
import functools

import jax
import jax.numpy as jnp
from jax import lax
from jax.experimental import pallas as pl
from jax.experimental.pallas import tpu as pltpu
from jax.sharding import PartitionSpec as P

MESH = pl.DeviceIdType.MESH
F32, BF16 = jnp.float32, jnp.bfloat16
LANES = 128
PIVOTS = 4
ROUNDS = 9
PITCH = 72


def harmonic(left_side, right_side):
    return 2.0 * left_side * right_side / (left_side + right_side)


def split(values):
    high = values.astype(BF16)
    return high, (values - high.astype(F32)).astype(BF16)


def dot_t(left, right):
    return lax.dot_general(left, right, (((1,), (1,)), ((), ())), preferred_element_type=F32)


def inverse(matrix):
    n = matrix.shape[0]
    row_id = lax.broadcasted_iota(jnp.int32, (n, n), 0)
    col_id = lax.broadcasted_iota(jnp.int32, (n, n), 1)
    work = jnp.concatenate([matrix, (row_id == col_id).astype(F32)], axis=1)
    wide_row = lax.broadcasted_iota(jnp.int32, work.shape, 0)
    for base in range(0, n, PIVOTS):
        ids = range(PIVOTS)
        rows = [work[base + i : base + i + 1, :] for i in ids]
        pivot = [
            [jnp.broadcast_to(rows[i][:, base + j : base + j + 1], rows[i].shape) for j in ids]
            for i in ids
        ]
        inside = (wide_row >= base) & (wide_row < base + PIVOTS)
        columns = [
            jnp.where(
                inside,
                jnp.where(wide_row == base + j, -1.0, 0.0),
                jnp.broadcast_to(work[:, base + j : base + j + 1], work.shape),
            )
            for j in ids
        ]
        work = jnp.where(inside, 0.0, work)
        for p in ids:
            scale = 1.0 / pivot[p][p]
            rows[p] = rows[p] * scale
            for j in range(p + 1, PIVOTS):
                pivot[p][j] = pivot[p][j] * scale
            for i in ids:
                if i != p:
                    factor = pivot[i][p]
                    rows[i] = rows[i] - factor * rows[p]
                    for j in range(p + 1, PIVOTS):
                        pivot[i][j] = pivot[i][j] - factor * pivot[p][j]
        for j in ids:
            work = work - columns[j] * rows[j]
    return work[:, n:]


def kernel(
    n_row, n_col,
    cap_ref, con_ref, par_ref, rhs_hbm, mat_hbm, vent_hbm, basis_hbm,
    x_ref, r_ref, e_ref,
    rhs_ref, mat_ref, vent_ref, basis_ref,
    fields, ysend, yrecv, info, zf, zk, zr, yb, az, xb, pa, pb, pc, coef, zo, work, wide, inv_ref,
    red_row, red_col, load,
    top_s, top_r, x_s, x_r, y_s, y_r, info_s, info_r, xb_s, xb_r, pa_s, pa_r, pc_s, pc_r,
    rr_s, rr_r, rc_s, rc_r, *tops,
):
    layers, width, depth = rhs_ref.shape
    vectors = basis_ref.shape[0]
    lines = layers * width
    share = width // n_row
    row, col = lax.axis_index("row"), lax.axis_index("col")
    row_up, row_dn = lax.rem(row + 1, n_row), lax.rem(row + n_row - 1, n_row)
    col_up, col_dn = lax.rem(col + 1, n_col), lax.rem(col + n_col - 1, n_col)

    order = sorted(range(1, n_row), key=lambda i: min(i, n_row - i), reverse=True)

    def peer(i, me, count):
        return lax.rem(me + i, count)

    def remote(src, dst, send, recv, target):
        return pltpu.make_async_remote_copy(
            src_ref=src, dst_ref=dst, send_sem=send, recv_sem=recv,
            device_id=target, device_id_type=MESH,
        )

    def wait_bytes(ref, sem):
        pltpu.make_async_copy(ref, ref, sem).wait()

    barrier = pltpu.get_barrier_semaphore()

    @pl.loop(1, n_row)
    def _(i):
        pl.semaphore_signal(
            barrier, inc=1, device_id=(peer(i, row, n_row), col), device_id_type=MESH
        )

    for neighbour in (col_up, col_dn):
        pl.semaphore_signal(barrier, inc=1, device_id=(row, neighbour), device_id_type=MESH)

    loads = [
        pltpu.make_async_copy(src, dst, load.at[i])
        for i, (src, dst) in enumerate(
            (
                (mat_hbm, mat_ref), (vent_hbm, vent_ref),
                (rhs_hbm, rhs_ref), (basis_hbm, basis_ref),
            )
        )
    ]
    for copy in loads:
        copy.start()
    for copy in loads[:2]:
        copy.wait()

    material = mat_ref[...]
    conduct = jnp.zeros(material.shape, F32)
    heat = jnp.zeros(material.shape, F32)
    for class_id in range(con_ref.shape[0]):
        hit = material == class_id
        conduct = jnp.where(hit, con_ref[class_id], conduct)
        heat = jnp.where(hit, cap_ref[class_id], heat)
    vent = vent_ref[...]
    partner = [par_ref[k] for k in range(2)]
    info_row = lax.broadcasted_iota(jnp.int32, (8, LANES), 0)
    info[row] = jnp.where(
        info_row == 0, partner[0].astype(F32), jnp.where(info_row == 1, partner[1].astype(F32), 0.0)
    )
    line_id = lax.broadcasted_iota(jnp.int32, (lines, depth), 0)
    lane_id = lax.broadcasted_iota(jnp.int32, (lines, depth), 1)
    on_first, on_last = lane_id == line_id, lane_id == line_id + lines

    def pack_sides(first, last):
        spread = jnp.where(on_first, first, 0.0) + jnp.where(on_last, last, 0.0)
        return jnp.sum(spread, axis=0, keepdims=True)

    def send_sides(at, packed):
        ysend[at] = jnp.broadcast_to(packed, (8, LANES))
        for copy in y_copies(at):
            copy.start()

    def send_top(at, top):
        tops[at][row] = top
        for i in order:
            remote(
                tops[at].at[row], tops[at].at[row], top_s.at[at], top_r.at[at],
                (peer(i, row, n_row), col),
            ).start()

    def send_lines(at, values):
        fields[at, :, 8 : 8 + width, :] = values
        for copy in x_copies(at):
            copy.start()

    def start_exchange(at, values, top):
        flat = values.reshape(lines, depth)
        send_sides(at, pack_sides(flat[:, 0:1], flat[:, depth - 1 : depth]))
        send_top(at, top)
        send_lines(at, values)

    def x_copies(at):
        return (
            remote(
                fields.at[at, :, pl.ds(7 + width, 1), :], fields.at[at, :, pl.ds(7, 1), :],
                x_s.at[at, 0], x_r.at[at, 0], (row_up, col),
            ),
            remote(
                fields.at[at, :, pl.ds(8, 1), :], fields.at[at, :, pl.ds(8 + width, 1), :],
                x_s.at[at, 1], x_r.at[at, 1], (row_dn, col),
            ),
        )

    def y_copies(at):
        return (
            remote(ysend.at[at], yrecv.at[at, 0], y_s.at[at, 0], y_r.at[at, 0], (row, col_up)),
            remote(ysend.at[at], yrecv.at[at, 1], y_s.at[at, 1], y_r.at[at, 1], (row, col_dn)),
        )

    def finish_exchange(at, values):
        for copy in x_copies(at):
            copy.wait_recv()
        wait_bytes(tops[at].at[pl.ds(0, n_row - 1)], top_r.at[at])
        for copy in y_copies(at):
            copy.wait_recv()
        flat = values.reshape(lines, depth)
        from_dn = jnp.where(on_last, yrecv[at, 0, 0:1, :], 0.0)
        from_up = jnp.where(on_first, yrecv[at, 1, 0:1, :], 0.0)
        dn_y = jnp.where(
            lane_id == 0, jnp.sum(from_dn, axis=1, keepdims=True), pltpu.roll(flat, 1, 1)
        ).reshape(values.shape)
        up_y = jnp.where(
            lane_id == depth - 1,
            jnp.sum(from_up, axis=1, keepdims=True),
            pltpu.roll(flat, depth - 1, 1),
        ).reshape(values.shape)
        dn_x = fields[at, :, 7 : 7 + width, :]
        up_x = fields[at, :, 9 : 9 + width, :]
        coupled = tops[at][partner[0]] + tops[at][partner[1]]
        return up_x, dn_x, up_y, dn_y, coupled

    pl.semaphore_wait(barrier, n_row - 1 + 2)
    start_exchange(0, conduct, vent)

    @pl.loop(1, n_row)
    def _(i):
        remote(info.at[row], info.at[row], info_s, info_r, (peer(i, row, n_row), col)).start()

    for copy in loads[2:]:
        copy.wait()

    @pl.loop(0, vectors)
    def _(a):
        zf[pl.ds(a * PITCH, lines), :] = basis_ref[a].astype(F32)

    zk[lines * vectors :, :] = jnp.zeros((width * vectors, depth), F32)

    def line(k):
        return pl.ds(k * vectors, vectors)

    basis_lane = lax.broadcasted_iota(jnp.int32, (vectors, depth), 1)

    def turn(k, sides):
        block = zf[pl.ds(k, vectors, stride=PITCH), :]
        zk[line(k), :] = block
        zr[:, pl.ds(pl.multiple_of(k * depth, depth), depth)] = block.astype(BF16)
        sides = jnp.where(basis_lane == k, block[:, 0:1], sides)
        return jnp.where(basis_lane == lines + k, block[:, depth - 1 : depth], sides)

    yb[...] = lax.fori_loop(0, lines, turn, jnp.zeros((vectors, depth), F32))

    def cells(k):
        return pl.ds(pl.multiple_of(k * depth, depth), depth)

    def face_copies():
        copies = []
        for z in range(layers):
            there = pl.ds(z * depth, depth)
            copies.append(
                remote(
                    zr.at[:, cells(z * width + width - 1)], xb.at[0, :, there],
                    xb_s.at[0, z], xb_r.at[0, z], (row_up, col),
                )
            )
            copies.append(
                remote(
                    zr.at[:, cells(z * width)], xb.at[1, :, there],
                    xb_s.at[1, z], xb_r.at[1, z], (row_dn, col),
                )
            )
        return copies

    top_line = (layers - 1) * width
    for copy in face_copies():
        copy.start()

    @pl.loop(1, n_row)
    def _(i):
        target = peer(i, row, n_row)
        first = top_line + target * share
        remote(
            zr.at[:, pl.ds(pl.multiple_of(first * depth, depth), share * depth)], pa.at[row],
            pa_s, pa_r, (target, col),
        ).start()

    def project(values):
        work[...] = values.reshape(lines, depth)

        def step(k, total):
            return total + zk[line(k), :] * work[pl.ds(k, 1), :]

        total = lax.fori_loop(0, lines, step, jnp.zeros((vectors, depth), F32), unroll=8)
        return jnp.sum(total, axis=1, keepdims=True)

    def expand(at, coarse):
        spread = jnp.broadcast_to(coarse, wide.shape)
        wide[...] = spread
        send_sides(at, jnp.sum(spread * yb[...], axis=0, keepdims=True))

        def part(first, count):
            def step(a, total):
                return total + zf[pl.ds(a * PITCH + first, count), :] * wide[pl.ds(a, 1), :]

            return lax.fori_loop(0, vectors, step, jnp.zeros((count, depth), F32), unroll=8)

        top = part(top_line, width)
        send_top(at, vent * top)
        rest = part(0, top_line)
        total = jnp.concatenate([rest, top], axis=0).reshape(layers, width, depth)
        send_lines(at, total)
        return total

    square_row = lax.broadcasted_iota(jnp.int32, (vectors, vectors), 0)
    square_col = lax.broadcasted_iota(jnp.int32, (vectors, vectors), 1)

    def solve(right_side):
        flat = jnp.sum(jnp.where(square_row == square_col, right_side, 0.0), axis=0, keepdims=True)
        return jnp.sum(inv_ref[...] * flat, axis=1, keepdims=True)

    rhs = rhs_ref[...]
    first_side = project(rhs)

    x_id = lax.broadcasted_iota(jnp.int32, conduct.shape, 1)
    y_id = lax.broadcasted_iota(jnp.int32, conduct.shape, 2)
    x_last, x_first = x_id == width - 1, x_id == 0
    y_last, y_first = y_id == depth - 1, y_id == 0
    none = jnp.zeros((1, width, depth), F32)
    up_z = jnp.concatenate([harmonic(conduct[:-1], conduct[1:]), none], axis=0)
    dn_z = jnp.concatenate([none, up_z[:-1]], axis=0)
    in_up_x = jnp.where(x_last, 0.0, harmonic(conduct, pltpu.roll(conduct, width - 1, 1)))
    in_dn_x = jnp.where(x_first, 0.0, pltpu.roll(in_up_x, 1, 1))
    in_up_y = jnp.where(y_last, 0.0, harmonic(conduct, pltpu.roll(conduct, depth - 1, 2)))
    in_dn_y = jnp.where(y_first, 0.0, pltpu.roll(in_up_y, 1, 2))
    inside = heat + up_z + dn_z + in_up_x + in_dn_x + in_up_y + in_dn_y
    for c, part in enumerate((0.5 * inside, up_z, in_up_x, in_up_y)):
        coef[c] = part.reshape(lines, depth)

    def keep(rows, where):
        high, low = split(rows)
        az[0:vectors, where] = high
        az[vectors : 2 * vectors, where] = low

    @pl.loop(0, lines)
    def _(k):
        own = zk[line(k), :]

        def at(c):
            return coef[c, pl.ds(k, 1), :]

        applied = at(0) * own - at(1) * zk[line(k + width), :]
        applied = applied - at(2) * zk[line(k + 1), :] - at(3) * pltpu.roll(own, depth - 1, 1)
        keep(applied, cells(k))

    half = dot_t(az[...], zr[...])
    half = half[:vectors] + half[vectors:]
    own_block = half + half.T

    near = finish_exchange(0, conduct)
    out_up_x = jnp.where(x_last & (row < n_row - 1), harmonic(conduct, near[0]), 0.0)
    out_dn_x = jnp.where(x_first & (row > 0), harmonic(conduct, near[1]), 0.0)
    out_up_y = jnp.where(y_last & (col < n_col - 1), harmonic(conduct, near[2]), 0.0)
    out_dn_y = jnp.where(y_first & (col > 0), harmonic(conduct, near[3]), 0.0)
    up_x, dn_x = in_up_x + out_up_x, in_dn_x + out_dn_x
    up_y, dn_y = in_up_y + out_up_y, in_dn_y + out_dn_y
    outside = jnp.concatenate(
        [(out_up_x + out_dn_x)[:-1], (out_up_x + out_dn_x)[-1:] + (vent * near[4])[None]], axis=0
    )
    diagonal = inside + outside + out_up_y + out_dn_y

    outer = [z * width + x for z in range(layers - 1) for x in (0, width - 1)]
    outer += list(range(top_line, lines))
    coef[4] = outside.reshape(lines, depth)
    for i, k in enumerate(outer):
        there = pl.ds(i * depth, depth)
        keep(coef[4, k : k + 1, :] * zk[line(k), :], there)
        zo[:, there] = zr[:, cells(k)]
    side_gain = pack_sides(
        out_dn_y.reshape(lines, depth)[:, 0:1], out_up_y.reshape(lines, depth)[:, depth - 1 : depth]
    )
    there = pl.ds(len(outer) * depth, depth)
    keep(side_gain * yb[...], there)
    zo[:, there] = yb[...].astype(BF16)
    size = (len(outer) + 1) * depth
    extra = dot_t(az[:, :size], zo[...])
    own_block = own_block + extra[:vectors] + extra[vectors:]
    inv_ref[...] = inverse(own_block)

    def apply_start(at, values):
        start_exchange(at, values, vent * values[layers - 1])

    def apply_finish(at, values):
        near = finish_exchange(at, values)
        none = jnp.zeros((1, width, depth), F32)
        result = diagonal * values
        result = result - up_z * jnp.concatenate([values[1:], none], axis=0)
        result = result - dn_z * jnp.concatenate([none, values[:-1]], axis=0)
        result = result - up_x * near[0] - dn_x * near[1] - up_y * near[2] - dn_y * near[3]
        return jnp.concatenate([result[:-1], (result[-1] - vent * near[4])[None]], axis=0)

    def apply(at, values, beside):
        apply_start(at, values)
        beside()
        return apply_finish(at, values)

    def apply_coarse(at, coarse, beside):
        values = expand(at, coarse)
        beside()
        return values, apply_finish(at, values)

    def correct(at, right_side, besides):
        first, first_image = apply_coarse(at, solve(right_side), besides[0])
        second, second_image = apply_coarse(
            at + 1, solve(right_side - project(first_image)), besides[1]
        )
        return first + second, first_image + second_image

    def faces():
        for copy in face_copies():
            copy.wait_recv()
        for side, at, coefficient in ((0, 0, dn_x), (1, width - 1, up_x)):
            terms = [
                zk[line(z * width + at), :] * coefficient[z, at : at + 1, :] for z in range(layers)
            ]
            high, low = split(jnp.concatenate(terms, axis=1))
            both = dot_t(jnp.concatenate([high, low], axis=0), xb[side])
            wide_faces[side] = both[:vectors] + both[vectors:]

    wide_faces = [None, None]
    third = n_row // 3

    def nothing():
        pass

    def begin():
        faces()
        plenum_start()
        plenum(0, third)

    def plenum_start():
        wait_bytes(info.at[pl.ds(0, n_row - 1)], info_r)
        wait_bytes(pa.at[pl.ds(0, n_row - 1)], pa_r)
        first = top_line + row * share
        pa[row] = zr[:, pl.ds(pl.multiple_of(first * depth, depth), share * depth)]

    def plenum(first, last):
        @pl.loop(first, last)
        def _(offset):
            s = peer(offset, row, n_row)
            own = pa[s]
            total = None
            for i in range(share):
                rows = []
                for k in range(2):
                    which = info[s, k : k + 1, :]
                    chosen = jnp.zeros((vectors, depth), F32)
                    gain = jnp.zeros((1, depth), F32)
                    for t in range(n_row):
                        block = pa[t, :, i * depth : (i + 1) * depth].astype(F32)
                        gain = jnp.where(which == t, tops[0][t, pl.ds(row * share + i, 1), :], gain)
                        chosen = jnp.where(which == t, block, chosen)
                    rows.append(chosen * (gain * tops[0][s, pl.ds(row * share + i, 1), :]))
                high, low = split(jnp.concatenate(rows, axis=0))
                mine = own[:, i * depth : (i + 1) * depth]
                part = dot_t(
                    jnp.concatenate([mine, mine], axis=1), jnp.concatenate([high, low], axis=1)
                )
                total = part if total is None else total + part
            pb[s] = total

            @pl.when(offset > 0)
            def _():
                remote(pb.at[s], pc.at[row], pc_s, pc_r, (s, col)).start()

            @pl.when(offset == 0)
            def _():
                pc[row] = pb[s]

    def finish_blocks():
        wait_bytes(pc.at[pl.ds(0, n_row - 1)], pc_r)
        total = lax.fori_loop(
            0, n_row, lambda i, t: t + pc[i], jnp.zeros((vectors, 2 * vectors), F32)
        )
        scale = 1.0 / (lines * depth)
        parts = (
            own_block * scale, wide_faces[0] * -scale, wide_faces[1] * -scale,
            total[:, :vectors] * -scale, total[:, vectors:] * -scale,
        )

        @pl.loop(0, n_row)
        def _(q):
            hits = (q == row, q == row - 1, q == row + 1, q == partner[0], q == partner[1])
            value = jnp.zeros((vectors, vectors), F32)
            for hit, part in zip(hits, parts):
                value = value + jnp.where(hit, 1.0, 0.0) * part
            e_ref[q] = value

    iterate, image = correct(
        1, first_side, (begin, lambda: plenum(third, 2 * third))
    )
    defect = rhs - image
    turned = apply(3, defect, lambda: plenum(2 * third, n_row))
    shift, image = correct(4, project(turned), (nothing, nothing))
    direction, stepped = defect - shift, turned - image
    turned = apply(6, stepped, finish_blocks)
    shift, image = correct(7, project(turned), (nothing, nothing))
    slanted, slanted_image = stepped - shift, turned - image

    def lanes_of(left, right):
        return jnp.sum((left * right).reshape(lines, depth), axis=0, keepdims=True)

    sums = [
        lanes_of(defect, defect), lanes_of(direction, stepped), lanes_of(defect, stepped),
        lanes_of(stepped, stepped), lanes_of(slanted, stepped), lanes_of(slanted, slanted_image),
    ]
    red_row[row] = jnp.concatenate(sums + [jnp.zeros((2, depth), F32)], axis=0)

    @pl.loop(1, n_row)
    def _(i):
        remote(red_row.at[row], red_row.at[row], rr_s, rr_r, (peer(i, row, n_row), col)).start()

    wait_bytes(red_row.at[pl.ds(0, n_row - 1)], rr_r)
    red_col[col] = jnp.sum(red_row[...], axis=0)

    @pl.loop(1, n_col)
    def _(i):
        remote(red_col.at[col], red_col.at[col], rc_s, rc_r, (row, peer(i, col, n_col))).start()

    wait_bytes(red_col.at[pl.ds(0, n_col - 1)], rc_r)
    scalars = jnp.sum(jnp.sum(red_col[...], axis=0), axis=1, keepdims=True)
    norm, curve, cross, square, mixed, slant = [scalars[i : i + 1, :] for i in range(6)]
    alpha = norm / curve
    after = norm - 2.0 * alpha * cross + alpha * alpha * square
    more = 1.0 + after / norm
    curve = more * more * curve - 2.0 * more * alpha * mixed + alpha * alpha * slant
    last = after / curve

    def scaled(factor, values):
        return jnp.broadcast_to(factor, values.shape) * values

    alpha, more, last = alpha[None], more[None], last[None]
    x_ref[...] = (
        iterate
        + scaled(alpha, direction)
        + scaled(last, scaled(more, direction) - scaled(alpha, slanted))
    )
    r_ref[...] = (
        defect
        - scaled(alpha, stepped)
        - scaled(last, scaled(more, stepped) - scaled(alpha, slanted_image))
    )

    for at in range(ROUNDS):
        for copy in x_copies(at) + y_copies(at):
            copy.wait_send()
        wait_bytes(tops[at].at[pl.ds(0, n_row - 1)], top_s.at[at])

    for copy in face_copies():
        copy.wait_send()
    wait_bytes(info.at[pl.ds(0, n_row - 1)], info_s)
    wait_bytes(pa.at[pl.ds(0, n_row - 1)], pa_s)
    wait_bytes(pc.at[pl.ds(0, n_row - 1)], pc_s)
    wait_bytes(red_row.at[pl.ds(0, n_row - 1)], rr_s)
    wait_bytes(red_col.at[pl.ds(0, n_col - 1)], rc_s)


def body(n_row, n_col, rhs, material, capacity, conductivity, vent, partners, basis):
    layers, width, depth = rhs.shape
    vectors = basis.shape[0]
    lines, share = layers * width, width // n_row
    smem, vmem = pl.BlockSpec(memory_space=pltpu.SMEM), pl.BlockSpec(memory_space=pltpu.VMEM)
    hbm = pl.BlockSpec(memory_space=pltpu.HBM)
    outer = 2 * (layers - 1) + width
    dma = pltpu.SemaphoreType.DMA
    scratch = [
        pltpu.VMEM(rhs.shape, F32), pltpu.VMEM(material.shape, jnp.int32),
        pltpu.VMEM(vent.shape, F32), pltpu.VMEM((vectors, lines, depth), BF16),
        pltpu.VMEM((ROUNDS, layers, width + 16, depth), F32),
        pltpu.VMEM((ROUNDS, 8, LANES), F32),
        pltpu.VMEM((ROUNDS, 2, 8, LANES), F32),
        pltpu.VMEM((n_row, 8, LANES), F32),
        pltpu.VMEM((vectors * PITCH, depth), F32),
        pltpu.VMEM((vectors * (lines + width), depth), F32),
        pltpu.VMEM((vectors, lines * depth), BF16),
        pltpu.VMEM((vectors, depth), F32),
        pltpu.VMEM((2 * vectors, lines * depth), BF16),
        pltpu.VMEM((2, vectors, layers * depth), BF16),
        pltpu.VMEM((n_row, vectors, share * depth), BF16),
        pltpu.VMEM((n_row, vectors, 2 * vectors), F32),
        pltpu.VMEM((n_row, vectors, 2 * vectors), F32),
        pltpu.VMEM((5, lines, depth), F32),
        pltpu.VMEM((vectors, (outer + 1) * depth), BF16),
        pltpu.VMEM((lines, depth), F32),
        pltpu.VMEM((vectors, depth), F32),
        pltpu.VMEM((vectors, vectors), F32),
        pltpu.VMEM((n_row, 8, LANES), F32),
        pltpu.VMEM((n_col, 8, LANES), F32),
        dma((4,)), dma((ROUNDS,)), dma((ROUNDS,)), dma((ROUNDS, 2)), dma((ROUNDS, 2)),
        dma((ROUNDS, 2)), dma((ROUNDS, 2)), dma, dma, dma((2, layers)), dma((2, layers)),
        dma, dma, dma, dma, dma, dma, dma, dma,
        *[pltpu.VMEM((n_row, width, depth), F32) for _ in range(ROUNDS)],
    ]
    iterate, defect, blocks = pl.pallas_call(
        functools.partial(kernel, n_row, n_col),
        out_shape=(
            jax.ShapeDtypeStruct(rhs.shape, F32),
            jax.ShapeDtypeStruct(rhs.shape, F32),
            jax.ShapeDtypeStruct((n_row, vectors, vectors), F32),
        ),
        in_specs=[smem, smem, smem, hbm, hbm, hbm, hbm],
        out_specs=(vmem, vmem, vmem),
        scratch_shapes=scratch,
        compiler_params=pltpu.CompilerParams(
            collective_id=0, has_side_effects=True, vmem_limit_bytes=48 * 1024 * 1024
        ),
        name="deflated_cg",
    )(
        capacity, conductivity, partners.reshape(-1), rhs, material, vent,
        basis.reshape(vectors, lines, depth),
    )
    return iterate, defect, blocks[None, None]


def solution(mesh):
    n_row, n_col = mesh.shape["row"], mesh.shape["col"]
    return jax.shard_map(
        functools.partial(body, n_row, n_col),
        mesh=mesh,
        in_specs=(
            P(None, "row", "col"),
            P(None, "row", "col"),
            P(),
            P(),
            P("row", "col"),
            P("row", "col", None),
            P(None, None, "row", "col"),
        ),
        out_specs=(P(None, "row", "col"), P(None, "row", "col"), P("row", "col", None, None, None)),
        check_vma=False,
    )
```

```python
import functools

import jax
import jax.numpy as jnp
from jax import lax
from jax.experimental import pallas as pl
from jax.experimental.pallas import tpu as pltpu
from jax.sharding import PartitionSpec as P

MESH = pl.DeviceIdType.MESH
F32, BF16 = jnp.float32, jnp.bfloat16
LANES = 128
PIVOTS = 4
ROUNDS = 9
PITCH = 72
COARSE_ROUNDS = (4, 7)


def harmonic(left_side, right_side):
    return 2.0 * left_side * right_side / (left_side + right_side)


def split(values):
    high = values.astype(BF16)
    return high, (values - high.astype(F32)).astype(BF16)


def dot_t(left, right):
    return lax.dot_general(left, right, (((1,), (1,)), ((), ())), preferred_element_type=F32)


def inverse(matrix):
    n = matrix.shape[0]
    row_id = lax.broadcasted_iota(jnp.int32, (n, n), 0)
    col_id = lax.broadcasted_iota(jnp.int32, (n, n), 1)
    work = jnp.concatenate([matrix, (row_id == col_id).astype(F32)], axis=1)
    wide_row = lax.broadcasted_iota(jnp.int32, work.shape, 0)
    for base in range(0, n, PIVOTS):
        ids = range(PIVOTS)
        rows = [work[base + i : base + i + 1, :] for i in ids]
        pivot = [
            [jnp.broadcast_to(rows[i][:, base + j : base + j + 1], rows[i].shape) for j in ids]
            for i in ids
        ]
        inside = (wide_row >= base) & (wide_row < base + PIVOTS)
        columns = [
            jnp.where(
                inside,
                jnp.where(wide_row == base + j, -1.0, 0.0),
                jnp.broadcast_to(work[:, base + j : base + j + 1], work.shape),
            )
            for j in ids
        ]
        work = jnp.where(inside, 0.0, work)
        for p in range(0, PIVOTS, 2):
            (a, b), (c, d) = (pivot[p + i][p : p + 2] for i in range(2))
            scale = 1.0 / (a * d - b * c)
            a, b, c, d = d * scale, -b * scale, -c * scale, a * scale
            rows[p], rows[p + 1] = a * rows[p] + b * rows[p + 1], c * rows[p] + d * rows[p + 1]
            for j in range(p + 2, PIVOTS):
                first, second = pivot[p][j], pivot[p + 1][j]
                pivot[p][j], pivot[p + 1][j] = a * first + b * second, c * first + d * second
            for i in ids:
                if i not in (p, p + 1):
                    first, second = pivot[i][p], pivot[i][p + 1]
                    rows[i] = rows[i] - (first * rows[p] + second * rows[p + 1])
                    for j in range(p + 2, PIVOTS):
                        pivot[i][j] = pivot[i][j] - (
                            first * pivot[p][j] + second * pivot[p + 1][j]
                        )
        for j in ids:
            work = work - columns[j] * rows[j]
    return work[:, n:]


def kernel(
    n_row, n_col,
    cap_ref, con_ref, par_ref, rhs_hbm, mat_hbm, vent_hbm, basis_hbm,
    x_ref, r_ref, e_ref,
    rhs_ref, mat_ref, vent_ref, basis_ref,
    fields, ysend, yrecv, info, zf, zk, zr, yb, ybs, ybr, eb, ysv, yrv, az, xb, pa, pb, pc, coef, zo, work, wide, inv_ref,
    red_row, red_col, load,
    top_s, top_r, x_s, x_r, y_s, y_r, info_s, info_r, yb_s, yb_r, xb_s, xb_r, pa_s, pa_r, pc_s, pc_r,
    rr_s, rr_r, rc_s, rc_r, *more,
):
    tops, coarse_rows = more[:ROUNDS], dict(zip(COARSE_ROUNDS, more[ROUNDS:]))
    layers, width, depth = rhs_ref.shape
    vectors = basis_ref.shape[0]
    lines = layers * width
    share = width // n_row
    row, col = lax.axis_index("row"), lax.axis_index("col")
    row_up, row_dn = lax.rem(row + 1, n_row), lax.rem(row + n_row - 1, n_row)
    col_up, col_dn = lax.rem(col + 1, n_col), lax.rem(col + n_col - 1, n_col)

    count_x = n_row // 4
    steps = [(dx, dy, dc) for dx in range(count_x) for dy in range(2) for dc in range(2)]
    steps = sorted(steps[1:], key=lambda s: (min(s[0], count_x - s[0]) + s[1], s), reverse=True)

    def peer(i, me, count):
        return lax.rem(me + i, count)

    def row_peers():
        x, rest = row // 4, lax.rem(row, 4)
        for dx, dy, dc in steps:
            yield (
                lax.rem(x + dx, count_x) * 4
                + lax.rem(rest // 2 + dy, 2) * 2
                + lax.rem(lax.rem(rest, 2) + dc, 2)
            )

    def remote(src, dst, send, recv, target):
        return pltpu.make_async_remote_copy(
            src_ref=src, dst_ref=dst, send_sem=send, recv_sem=recv,
            device_id=target, device_id_type=MESH,
        )

    def wait_bytes(ref, sem):
        pltpu.make_async_copy(ref, ref, sem).wait()

    barrier = pltpu.get_barrier_semaphore()

    @pl.loop(1, n_row)
    def _(i):
        pl.semaphore_signal(
            barrier, inc=1, device_id=(peer(i, row, n_row), col), device_id_type=MESH
        )

    for neighbour in (col_up, col_dn):
        pl.semaphore_signal(barrier, inc=1, device_id=(row, neighbour), device_id_type=MESH)

    loads = [
        pltpu.make_async_copy(src, dst, load.at[i])
        for i, (src, dst) in enumerate(
            (
                (mat_hbm, mat_ref), (vent_hbm, vent_ref),
                (rhs_hbm, rhs_ref), (basis_hbm, basis_ref),
            )
        )
    ]
    for copy in loads:
        copy.start()
    for copy in loads[:2]:
        copy.wait()

    material = mat_ref[...]
    conduct = jnp.zeros(material.shape, F32)
    heat = jnp.zeros(material.shape, F32)
    for class_id in range(con_ref.shape[0]):
        hit = material == class_id
        conduct = jnp.where(hit, con_ref[class_id], conduct)
        heat = jnp.where(hit, cap_ref[class_id], heat)
    vent = vent_ref[...]
    partner = [par_ref[k] for k in range(2)]
    info_row = lax.broadcasted_iota(jnp.int32, (8, LANES), 0)
    info[row] = jnp.where(
        info_row == 0, partner[0].astype(F32), jnp.where(info_row == 1, partner[1].astype(F32), 0.0)
    )
    line_id = lax.broadcasted_iota(jnp.int32, (lines, depth), 0)
    lane_id = lax.broadcasted_iota(jnp.int32, (lines, depth), 1)
    on_first, on_last = lane_id == line_id, lane_id == line_id + lines

    def pack_sides(first, last):
        spread = jnp.where(on_first, first, 0.0) + jnp.where(on_last, last, 0.0)
        return jnp.sum(spread, axis=0, keepdims=True)

    def send_sides(at, packed):
        ysend[at] = jnp.broadcast_to(packed, (8, LANES))
        for copy in y_copies(at):
            copy.start()

    def send_top(at, top):
        tops[at][row] = top
        for other in row_peers():
            remote(
                tops[at].at[row], tops[at].at[row], top_s.at[at], top_r.at[at], (other, col)
            ).start()

    def send_lines(at, values):
        fields[at, :, 8 : 8 + width, :] = values
        for copy in x_copies(at):
            copy.start()

    def start_exchange(at, values, top):
        flat = values.reshape(lines, depth)
        send_sides(at, pack_sides(flat[:, 0:1], flat[:, depth - 1 : depth]))
        send_top(at, top)
        send_lines(at, values)

    def x_copies(at):
        return (
            remote(
                fields.at[at, :, pl.ds(7 + width, 1), :], fields.at[at, :, pl.ds(7, 1), :],
                x_s.at[at, 0], x_r.at[at, 0], (row_up, col),
            ),
            remote(
                fields.at[at, :, pl.ds(8, 1), :], fields.at[at, :, pl.ds(8 + width, 1), :],
                x_s.at[at, 1], x_r.at[at, 1], (row_dn, col),
            ),
        )

    def y_copies(at):
        return (
            remote(ysend.at[at], yrecv.at[at, 0], y_s.at[at, 0], y_r.at[at, 0], (row, col_up)),
            remote(ysend.at[at], yrecv.at[at, 1], y_s.at[at, 1], y_r.at[at, 1], (row, col_dn)),
        )

    def finish_exchange(at, values):
        for copy in x_copies(at):
            copy.wait_recv()
        wait_bytes(tops[at].at[pl.ds(0, n_row - 1)], top_r.at[at])
        for copy in y_copies(at):
            copy.wait_recv()
        flat = values.reshape(lines, depth)
        from_dn = jnp.where(on_last, yrecv[at, 0, 0:1, :], 0.0)
        from_up = jnp.where(on_first, yrecv[at, 1, 0:1, :], 0.0)
        dn_y = jnp.where(
            lane_id == 0, jnp.sum(from_dn, axis=1, keepdims=True), pltpu.roll(flat, 1, 1)
        ).reshape(values.shape)
        up_y = jnp.where(
            lane_id == depth - 1,
            jnp.sum(from_up, axis=1, keepdims=True),
            pltpu.roll(flat, depth - 1, 1),
        ).reshape(values.shape)
        dn_x = fields[at, :, 7 : 7 + width, :]
        up_x = fields[at, :, 9 : 9 + width, :]
        coupled = tops[at][partner[0]] + tops[at][partner[1]]
        return up_x, dn_x, up_y, dn_y, coupled

    pl.semaphore_wait(barrier, n_row - 1 + 2)
    start_exchange(0, conduct, vent)

    @pl.loop(1, n_row)
    def _(i):
        remote(info.at[row], info.at[row], info_s, info_r, (peer(i, row, n_row), col)).start()

    for copy in loads[2:]:
        copy.wait()

    @pl.loop(0, vectors)
    def _(a):
        zf[pl.ds(a * PITCH, lines), :] = basis_ref[a].astype(F32)

    zk[lines * vectors :, :] = jnp.zeros((width * vectors, depth), F32)

    def line(k):
        return pl.ds(k * vectors, vectors)

    basis_lane = lax.broadcasted_iota(jnp.int32, (vectors, depth), 1)

    def turn(k, sides):
        block = zf[pl.ds(k, vectors, stride=PITCH), :]
        zk[line(k), :] = block
        zr[:, pl.ds(pl.multiple_of(k * depth, depth), depth)] = block.astype(BF16)
        sides = jnp.where(basis_lane == k, block[:, 0:1], sides)
        return jnp.where(basis_lane == lines + k, block[:, depth - 1 : depth], sides)

    yb[...] = lax.fori_loop(0, lines, turn, jnp.zeros((vectors, depth), F32))
    ybs[...] = yb[...].astype(BF16)
    side_basis = (
        remote(ybs, ybr.at[0], yb_s.at[0], yb_r.at[0], (row, col_up)),
        remote(ybs, ybr.at[1], yb_s.at[1], yb_r.at[1], (row, col_dn)),
    )

    def cells(k):
        return pl.ds(pl.multiple_of(k * depth, depth), depth)

    def face_copies():
        copies = []
        for z in range(layers):
            there = pl.ds(z * depth, depth)
            copies.append(
                remote(
                    zr.at[:, cells(z * width + width - 1)], xb.at[0, :, there],
                    xb_s.at[0, z], xb_r.at[0, z], (row_up, col),
                )
            )
            copies.append(
                remote(
                    zr.at[:, cells(z * width)], xb.at[1, :, there],
                    xb_s.at[1, z], xb_r.at[1, z], (row_dn, col),
                )
            )
        return copies

    top_line = (layers - 1) * width
    for copy in face_copies() + list(side_basis):
        copy.start()

    @pl.loop(1, n_row)
    def _(i):
        target = peer(i, row, n_row)
        first = top_line + target * share
        remote(
            zr.at[:, pl.ds(pl.multiple_of(first * depth, depth), share * depth)], pa.at[row],
            pa_s, pa_r, (target, col),
        ).start()

    def project(values):
        work[...] = values.reshape(lines, depth)

        def step(k, total):
            return total + zk[line(k), :] * work[pl.ds(k, 1), :]

        total = lax.fori_loop(0, lines, step, jnp.zeros((vectors, depth), F32), unroll=8)
        return jnp.sum(total, axis=1, keepdims=True)

    def expand(at, coarse):
        spread = jnp.broadcast_to(coarse, wide.shape)
        wide[...] = spread
        send_sides(at, jnp.sum(spread * yb[...], axis=0, keepdims=True))

        def part(first, count):
            def step(a, total):
                return total + zf[pl.ds(a * PITCH + first, count), :] * wide[pl.ds(a, 1), :]

            return lax.fori_loop(0, vectors, step, jnp.zeros((count, depth), F32), unroll=8)

        top = part(top_line, width)
        send_top(at, vent * top)
        rest = part(0, top_line)
        total = jnp.concatenate([rest, top], axis=0).reshape(layers, width, depth)
        send_lines(at, total)
        return total

    square_row = lax.broadcasted_iota(jnp.int32, (vectors, vectors), 0)
    square_col = lax.broadcasted_iota(jnp.int32, (vectors, vectors), 1)

    def solve(right_side):
        flat = jnp.sum(jnp.where(square_row == square_col, right_side, 0.0), axis=0, keepdims=True)
        return jnp.sum(inv_ref[...] * flat, axis=1, keepdims=True)

    rhs = rhs_ref[...]
    first_side = project(rhs)

    x_id = lax.broadcasted_iota(jnp.int32, conduct.shape, 1)
    y_id = lax.broadcasted_iota(jnp.int32, conduct.shape, 2)
    x_last, x_first = x_id == width - 1, x_id == 0
    y_last, y_first = y_id == depth - 1, y_id == 0
    none = jnp.zeros((1, width, depth), F32)
    up_z = jnp.concatenate([harmonic(conduct[:-1], conduct[1:]), none], axis=0)
    dn_z = jnp.concatenate([none, up_z[:-1]], axis=0)
    in_up_x = jnp.where(x_last, 0.0, harmonic(conduct, pltpu.roll(conduct, width - 1, 1)))
    in_dn_x = jnp.where(x_first, 0.0, pltpu.roll(in_up_x, 1, 1))
    in_up_y = jnp.where(y_last, 0.0, harmonic(conduct, pltpu.roll(conduct, depth - 1, 2)))
    in_dn_y = jnp.where(y_first, 0.0, pltpu.roll(in_up_y, 1, 2))
    inside = heat + up_z + dn_z + in_up_x + in_dn_x + in_up_y + in_dn_y
    for c, part in enumerate((0.5 * inside, up_z, in_up_x, in_up_y)):
        coef[c] = part.reshape(lines, depth)

    def keep(rows, where):
        high, low = split(rows)
        az[0:vectors, where] = high
        az[vectors : 2 * vectors, where] = low

    @pl.loop(0, lines)
    def _(k):
        own = zk[line(k), :]

        def at(c):
            return coef[c, pl.ds(k, 1), :]

        applied = at(0) * own - at(1) * zk[line(k + width), :]
        applied = applied - at(2) * zk[line(k + 1), :] - at(3) * pltpu.roll(own, depth - 1, 1)
        keep(applied, cells(k))

    half = dot_t(az[...], zr[...])
    half = half[:vectors] + half[vectors:]
    own_block = half + half.T

    near = finish_exchange(0, conduct)
    out_up_x = jnp.where(x_last & (row < n_row - 1), harmonic(conduct, near[0]), 0.0)
    out_dn_x = jnp.where(x_first & (row > 0), harmonic(conduct, near[1]), 0.0)
    out_up_y = jnp.where(y_last & (col < n_col - 1), harmonic(conduct, near[2]), 0.0)
    out_dn_y = jnp.where(y_first & (col > 0), harmonic(conduct, near[3]), 0.0)
    up_x, dn_x = in_up_x + out_up_x, in_dn_x + out_dn_x
    up_y, dn_y = in_up_y + out_up_y, in_dn_y + out_dn_y
    outside = jnp.concatenate(
        [(out_up_x + out_dn_x)[:-1], (out_up_x + out_dn_x)[-1:] + (vent * near[4])[None]], axis=0
    )
    diagonal = inside + outside + out_up_y + out_dn_y

    outer = [z * width + x for z in range(layers - 1) for x in (0, width - 1)]
    outer += list(range(top_line, lines))
    coef[4] = outside.reshape(lines, depth)
    for i, k in enumerate(outer):
        there = pl.ds(i * depth, depth)
        keep(coef[4, k : k + 1, :] * zk[line(k), :], there)
        zo[:, there] = zr[:, cells(k)]
    side_gain = pack_sides(
        out_dn_y.reshape(lines, depth)[:, 0:1], out_up_y.reshape(lines, depth)[:, depth - 1 : depth]
    )
    there = pl.ds(len(outer) * depth, depth)
    keep(side_gain * yb[...], there)
    zo[:, there] = yb[...].astype(BF16)
    size = (len(outer) + 1) * depth
    extra = dot_t(az[:, :size], zo[...])
    own_block = own_block + extra[:vectors] + extra[vectors:]
    inv_ref[...] = inverse(own_block)

    def apply_start(at, values):
        start_exchange(at, values, vent * values[layers - 1])

    def apply_finish(at, values):
        near = finish_exchange(at, values)
        none = jnp.zeros((1, width, depth), F32)
        result = diagonal * values
        result = result - up_z * jnp.concatenate([values[1:], none], axis=0)
        result = result - dn_z * jnp.concatenate([none, values[:-1]], axis=0)
        result = result - up_x * near[0] - dn_x * near[1] - up_y * near[2] - dn_y * near[3]
        return jnp.concatenate([result[:-1], (result[-1] - vent * near[4])[None]], axis=0)

    def apply(at, values, beside):
        apply_start(at, values)
        beside()
        return apply_finish(at, values)

    def apply_coarse(at, coarse, beside):
        values = expand(at, coarse)
        beside()
        return values, apply_finish(at, values)

    def correct(at, right_side, besides):
        first, first_image = apply_coarse(at, solve(right_side), besides[0])
        second, second_image = apply_coarse(
            at + 1, solve(right_side - project(first_image)), besides[1]
        )
        return first + second, first_image + second_image

    def coarse_copies(at):
        i = COARSE_ROUNDS.index(at)
        return (
            remote(ysv.at[i], yrv.at[i, 0], y_s.at[at, 0], y_r.at[at, 0], (row, col_up)),
            remote(ysv.at[i], yrv.at[i, 1], y_s.at[at, 1], y_r.at[at, 1], (row, col_dn)),
        )

    def correct_by_blocks(at, right_side, besides):
        coarse = solve(right_side)
        i, held = COARSE_ROUNDS.index(at), coarse_rows[at]
        packed = jnp.broadcast_to(pack_sides(coarse, coarse), (8, LANES))
        ysv[i] = packed
        held[row] = packed
        for copy in coarse_copies(at):
            copy.start()
        mine = held.at[row, pl.ds(0, 1)]
        for other in row_peers():
            remote(mine, mine, top_s.at[at], top_r.at[at], (other, col)).start()
        besides[0]()
        for copy in coarse_copies(at):
            copy.wait_recv()
        wait_bytes(held.at[pl.ds(0, n_row - 1), pl.ds(0, 1)], top_r.at[at])
        first_half = lax.broadcasted_iota(jnp.int32, (1, LANES), 1) < vectors
        pairs = (
            (held[row_dn, 0:1], held[row_up, 0:1]),
            (yrv[i, 0, 0:1], yrv[i, 1, 0:1]),
            (held[partner[0], 0:1], held[partner[1], 0:1]),
        )
        total = jnp.zeros((vectors, 2 * vectors), F32)
        for pair, (left, right) in enumerate(pairs):
            total = total + eb[pair] * jnp.where(first_half, left, right)
        coarse = coarse - solve(jnp.sum(total, axis=1, keepdims=True))
        return apply_coarse(at + 1, coarse, besides[1])

    def faces():
        for copy in face_copies() + list(side_basis):
            copy.wait_recv()
        halves = [pltpu.roll(ybr[side].astype(F32), depth - lines, 1) for side in range(2)]
        high, low = split(side_gain * yb[...])
        both = dot_t(
            jnp.concatenate([high, low], axis=0),
            jnp.concatenate(
                [
                    jnp.where(basis_lane < lines, halves[0], 0.0),
                    jnp.where(basis_lane < lines, 0.0, halves[1]),
                ],
                axis=0,
            ).astype(BF16),
        )
        eb[1] = -(both[:vectors] + both[vectors:])
        for side, at, coefficient in ((0, 0, dn_x), (1, width - 1, up_x)):
            terms = [
                zk[line(z * width + at), :] * coefficient[z, at : at + 1, :] for z in range(layers)
            ]
            high, low = split(jnp.concatenate(terms, axis=1))
            both = dot_t(jnp.concatenate([high, low], axis=0), xb[side])
            wide_faces[side] = both[:vectors] + both[vectors:]

    wide_faces = [None, None]

    def couplings():
        eb[0] = -jnp.concatenate(wide_faces, axis=1)
        wait_bytes(pc.at[pl.ds(0, n_row - 1)], pc_r)
        eb[2] = -lax.fori_loop(
            0, n_row, lambda i, t: t + pc[i], jnp.zeros((vectors, 2 * vectors), F32)
        )

    third = n_row // 3

    def nothing():
        pass

    def begin():
        faces()
        plenum_start()
        plenum(0, third)

    def plenum_start():
        wait_bytes(info.at[pl.ds(0, n_row - 1)], info_r)
        wait_bytes(pa.at[pl.ds(0, n_row - 1)], pa_r)
        first = top_line + row * share
        pa[row] = zr[:, pl.ds(pl.multiple_of(first * depth, depth), share * depth)]

    def plenum(first, last):
        @pl.loop(first, last)
        def _(offset):
            s = peer(offset, row, n_row)
            own = pa[s]
            total = None
            for i in range(share):
                rows = []
                for k in range(2):
                    which = info[s, k : k + 1, :]
                    chosen = jnp.zeros((vectors, depth), F32)
                    gain = jnp.zeros((1, depth), F32)
                    for t in range(n_row):
                        block = pa[t, :, i * depth : (i + 1) * depth].astype(F32)
                        gain = jnp.where(which == t, tops[0][t, pl.ds(row * share + i, 1), :], gain)
                        chosen = jnp.where(which == t, block, chosen)
                    rows.append(chosen * (gain * tops[0][s, pl.ds(row * share + i, 1), :]))
                high, low = split(jnp.concatenate(rows, axis=0))
                mine = own[:, i * depth : (i + 1) * depth]
                part = dot_t(
                    jnp.concatenate([mine, mine], axis=1), jnp.concatenate([high, low], axis=1)
                )
                total = part if total is None else total + part
            pb[s] = total

            @pl.when(offset > 0)
            def _():
                remote(pb.at[s], pc.at[row], pc_s, pc_r, (s, col)).start()

            @pl.when(offset == 0)
            def _():
                pc[row] = pb[s]

    def finish_blocks():
        scale = 1.0 / (lines * depth)
        parts = (
            own_block * scale, eb[0, :, :vectors] * scale, eb[0, :, vectors:] * scale,
            eb[2, :, :vectors] * scale, eb[2, :, vectors:] * scale,
        )

        @pl.loop(0, n_row)
        def _(q):
            hits = (q == row, q == row - 1, q == row + 1, q == partner[0], q == partner[1])
            value = jnp.zeros((vectors, vectors), F32)
            for hit, part in zip(hits, parts):
                value = value + jnp.where(hit, 1.0, 0.0) * part
            e_ref[q] = value

    iterate, image = correct(
        1, first_side, (begin, lambda: plenum(third, 2 * third))
    )
    defect = rhs - image
    turned = apply(3, defect, lambda: plenum(2 * third, n_row))
    shift, image = correct_by_blocks(4, project(turned), (couplings, nothing))
    direction, stepped = defect - shift, turned - image
    turned = apply(6, stepped, finish_blocks)
    shift, image = correct_by_blocks(7, project(turned), (nothing, nothing))
    slanted, slanted_image = stepped - shift, turned - image

    def lanes_of(left, right):
        return jnp.sum((left * right).reshape(lines, depth), axis=0, keepdims=True)

    sums = [
        lanes_of(defect, defect), lanes_of(direction, stepped), lanes_of(defect, stepped),
        lanes_of(stepped, stepped), lanes_of(slanted, stepped), lanes_of(slanted, slanted_image),
    ]
    sums = jnp.concatenate(sums + [jnp.zeros((2, depth), F32)], axis=0)
    scalar_at = lax.broadcasted_iota(jnp.int32, (8, LANES), 0) == lax.broadcasted_iota(
        jnp.int32, (8, LANES), 1
    )
    sums = jnp.where(scalar_at, jnp.sum(sums, axis=1, keepdims=True), 0.0)
    red_row[row] = jnp.sum(sums, axis=0, keepdims=True)
    for other in row_peers():
        remote(red_row.at[row], red_row.at[row], rr_s, rr_r, (other, col)).start()
    wait_bytes(red_row.at[pl.ds(0, n_row - 1)], rr_r)
    red_col[col] = jnp.sum(red_row[...], axis=0)
    ring = n_col // 2
    for i in sorted(range(1, n_col), key=lambda i: min(i % ring, ring - i % ring), reverse=True):
        remote(red_col.at[col], red_col.at[col], rc_s, rc_r, (row, peer(i, col, n_col))).start()
    wait_bytes(red_col.at[pl.ds(0, n_col - 1)], rc_r)
    scalars = jnp.where(scalar_at, jnp.sum(red_col[...], axis=0), 0.0)
    scalars = jnp.sum(scalars, axis=1, keepdims=True)
    norm, curve, cross, square, mixed, slant = [scalars[i : i + 1, :] for i in range(6)]
    alpha = norm / curve
    after = norm - 2.0 * alpha * cross + alpha * alpha * square
    gain = 1.0 + after / norm
    curve = gain * gain * curve - 2.0 * gain * alpha * mixed + alpha * alpha * slant
    last = after / curve

    def scaled(factor, values):
        return jnp.broadcast_to(factor, values.shape) * values

    alpha, gain, last = alpha[None], gain[None], last[None]
    x_ref[...] = (
        iterate
        + scaled(alpha, direction)
        + scaled(last, scaled(gain, direction) - scaled(alpha, slanted))
    )
    r_ref[...] = (
        defect
        - scaled(alpha, stepped)
        - scaled(last, scaled(gain, stepped) - scaled(alpha, slanted_image))
    )

    for at in range(ROUNDS):
        if at in COARSE_ROUNDS:
            for copy in coarse_copies(at):
                copy.wait_send()
            wait_bytes(coarse_rows[at].at[pl.ds(0, n_row - 1), pl.ds(0, 1)], top_s.at[at])
        else:
            for copy in x_copies(at) + y_copies(at):
                copy.wait_send()
            wait_bytes(tops[at].at[pl.ds(0, n_row - 1)], top_s.at[at])

    for copy in face_copies() + list(side_basis):
        copy.wait_send()
    wait_bytes(info.at[pl.ds(0, n_row - 1)], info_s)
    wait_bytes(pa.at[pl.ds(0, n_row - 1)], pa_s)
    wait_bytes(pc.at[pl.ds(0, n_row - 1)], pc_s)
    wait_bytes(red_row.at[pl.ds(0, n_row - 1)], rr_s)
    wait_bytes(red_col.at[pl.ds(0, n_col - 1)], rc_s)


def body(n_row, n_col, rhs, material, capacity, conductivity, vent, partners, basis):
    layers, width, depth = rhs.shape
    vectors = basis.shape[0]
    lines, share = layers * width, width // n_row
    smem, vmem = pl.BlockSpec(memory_space=pltpu.SMEM), pl.BlockSpec(memory_space=pltpu.VMEM)
    hbm = pl.BlockSpec(memory_space=pltpu.HBM)
    outer = 2 * (layers - 1) + width
    dma = pltpu.SemaphoreType.DMA
    scratch = [
        pltpu.VMEM(rhs.shape, F32), pltpu.VMEM(material.shape, jnp.int32),
        pltpu.VMEM(vent.shape, F32), pltpu.VMEM((vectors, lines, depth), BF16),
        pltpu.VMEM((ROUNDS, layers, width + 16, depth), F32),
        pltpu.VMEM((ROUNDS, 8, LANES), F32),
        pltpu.VMEM((ROUNDS, 2, 8, LANES), F32),
        pltpu.VMEM((n_row, 8, LANES), F32),
        pltpu.VMEM((vectors * PITCH, depth), F32),
        pltpu.VMEM((vectors * (lines + width), depth), F32),
        pltpu.VMEM((vectors, lines * depth), BF16),
        pltpu.VMEM((vectors, depth), F32),
        pltpu.VMEM((vectors, depth), BF16),
        pltpu.VMEM((2, vectors, depth), BF16),
        pltpu.VMEM((3, vectors, 2 * vectors), F32),
        pltpu.VMEM((len(COARSE_ROUNDS), 8, LANES), F32),
        pltpu.VMEM((len(COARSE_ROUNDS), 2, 8, LANES), F32),
        pltpu.VMEM((2 * vectors, lines * depth), BF16),
        pltpu.VMEM((2, vectors, layers * depth), BF16),
        pltpu.VMEM((n_row, vectors, share * depth), BF16),
        pltpu.VMEM((n_row, vectors, 2 * vectors), F32),
        pltpu.VMEM((n_row, vectors, 2 * vectors), F32),
        pltpu.VMEM((5, lines, depth), F32),
        pltpu.VMEM((vectors, (outer + 1) * depth), BF16),
        pltpu.VMEM((lines, depth), F32),
        pltpu.VMEM((vectors, depth), F32),
        pltpu.VMEM((vectors, vectors), F32),
        pltpu.VMEM((n_row, 1, LANES), F32),
        pltpu.VMEM((n_col, 1, LANES), F32),
        dma((4,)), dma((ROUNDS,)), dma((ROUNDS,)), dma((ROUNDS, 2)), dma((ROUNDS, 2)),
        dma((ROUNDS, 2)), dma((ROUNDS, 2)), dma, dma, dma((2,)), dma((2,)), dma((2, layers)), dma((2, layers)),
        dma, dma, dma, dma, dma, dma, dma, dma,
        *[pltpu.VMEM((n_row, width, depth), F32) for _ in range(ROUNDS)],
        *[pltpu.VMEM((n_row, 8, LANES), F32) for _ in COARSE_ROUNDS],
    ]
    iterate, defect, blocks = pl.pallas_call(
        functools.partial(kernel, n_row, n_col),
        out_shape=(
            jax.ShapeDtypeStruct(rhs.shape, F32),
            jax.ShapeDtypeStruct(rhs.shape, F32),
            jax.ShapeDtypeStruct((n_row, vectors, vectors), F32),
        ),
        in_specs=[smem, smem, smem, hbm, hbm, hbm, hbm],
        out_specs=(vmem, vmem, vmem),
        scratch_shapes=scratch,
        compiler_params=pltpu.CompilerParams(
            collective_id=0, has_side_effects=True, vmem_limit_bytes=67043328
        ),
        name="deflated_cg",
    )(
        capacity, conductivity, partners.reshape(-1), rhs, material, vent,
        basis.reshape(vectors, lines, depth),
    )
    return iterate, defect, blocks[None, None]


def solution(mesh):
    n_row, n_col = mesh.shape["row"], mesh.shape["col"]
    return jax.shard_map(
        functools.partial(body, n_row, n_col),
        mesh=mesh,
        in_specs=(
            P(None, "row", "col"),
            P(None, "row", "col"),
            P(),
            P(),
            P("row", "col"),
            P("row", "col", None),
            P(None, None, "row", "col"),
        ),
        out_specs=(P(None, "row", "col"), P(None, "row", "col"), P("row", "col", None, None, None)),
        check_vma=False,
    )
```

```python
import functools

import jax
import jax.numpy as jnp
from jax import lax
from jax.experimental import pallas as pl
from jax.experimental.pallas import tpu as pltpu
from jax.sharding import PartitionSpec as P

MESH = pl.DeviceIdType.MESH
F32, BF16 = jnp.float32, jnp.bfloat16
LANES = 128
PIVOTS = 4
ROUNDS = 9
PITCH = 72
COARSE_ROUNDS = (4, 7)


def harmonic(left_side, right_side):
    return 2.0 * left_side * right_side / (left_side + right_side)


def split(values):
    high = values.astype(BF16)
    return high, (values - high.astype(F32)).astype(BF16)


def dot_t(left, right):
    return lax.dot_general(left, right, (((1,), (1,)), ((), ())), preferred_element_type=F32)


def inverse(matrix):
    n = matrix.shape[0]
    row_id = lax.broadcasted_iota(jnp.int32, (n, n), 0)
    col_id = lax.broadcasted_iota(jnp.int32, (n, n), 1)
    work = jnp.concatenate([matrix, (row_id == col_id).astype(F32)], axis=1)
    wide_row = lax.broadcasted_iota(jnp.int32, work.shape, 0)
    for base in range(0, n, PIVOTS):
        ids = range(PIVOTS)
        rows = [work[base + i : base + i + 1, :] for i in ids]
        pivot = [
            [jnp.broadcast_to(rows[i][:, base + j : base + j + 1], rows[i].shape) for j in ids]
            for i in ids
        ]
        inside = (wide_row >= base) & (wide_row < base + PIVOTS)
        columns = [
            jnp.where(
                inside,
                jnp.where(wide_row == base + j, -1.0, 0.0),
                jnp.broadcast_to(work[:, base + j : base + j + 1], work.shape),
            )
            for j in ids
        ]
        work = jnp.where(inside, 0.0, work)
        for p in range(0, PIVOTS, 2):
            (a, b), (c, d) = (pivot[p + i][p : p + 2] for i in range(2))
            scale = 1.0 / (a * d - b * c)
            a, b, c, d = d * scale, -b * scale, -c * scale, a * scale
            rows[p], rows[p + 1] = a * rows[p] + b * rows[p + 1], c * rows[p] + d * rows[p + 1]
            for j in range(p + 2, PIVOTS):
                first, second = pivot[p][j], pivot[p + 1][j]
                pivot[p][j], pivot[p + 1][j] = a * first + b * second, c * first + d * second
            for i in ids:
                if i not in (p, p + 1):
                    first, second = pivot[i][p], pivot[i][p + 1]
                    rows[i] = rows[i] - (first * rows[p] + second * rows[p + 1])
                    for j in range(p + 2, PIVOTS):
                        pivot[i][j] = pivot[i][j] - (
                            first * pivot[p][j] + second * pivot[p + 1][j]
                        )
        for j in ids:
            work = work - columns[j] * rows[j]
    return work[:, n:]


def kernel(
    n_row, n_col,
    cap_ref, con_ref, par_ref, rhs_hbm, mat_hbm, vent_hbm, basis_hbm,
    x_ref, r_ref, e_ref,
    rhs_ref, mat_ref, vent_ref, basis_ref,
    fields, ysend, yrecv, info, zf, zk, zr, yb, ybs, ybr, eb, ysv, yrv, az, xb, pa, pb, pc, coef, zo, work, wide, inv_ref,
    red_row, red_col, load,
    top_s, top_r, x_s, x_r, y_s, y_r, info_s, info_r, yb_s, yb_r, xb_s, xb_r, pa_s, pa_r, pc_s, pc_r,
    rr_s, rr_r, rc_s, rc_r, *more,
):
    tops, coarse_rows = more[:ROUNDS], dict(zip(COARSE_ROUNDS, more[ROUNDS:]))
    layers, width, depth = rhs_ref.shape
    vectors = basis_ref.shape[0]
    lines = layers * width
    share = width // n_row
    row, col = lax.axis_index("row"), lax.axis_index("col")
    row_up, row_dn = lax.rem(row + 1, n_row), lax.rem(row + n_row - 1, n_row)
    col_up, col_dn = lax.rem(col + 1, n_col), lax.rem(col + n_col - 1, n_col)

    count_x = n_row // 4
    steps = [(dx, dy, dc) for dx in range(count_x) for dy in range(2) for dc in range(2)]
    steps = sorted(steps[1:], key=lambda s: (min(s[0], count_x - s[0]) + s[1], s), reverse=True)

    def peer(i, me, count):
        return lax.rem(me + i, count)

    def row_peers():
        x, rest = row // 4, lax.rem(row, 4)
        for dx, dy, dc in steps:
            yield (
                lax.rem(x + dx, count_x) * 4
                + lax.rem(rest // 2 + dy, 2) * 2
                + lax.rem(lax.rem(rest, 2) + dc, 2)
            )

    def remote(src, dst, send, recv, target):
        return pltpu.make_async_remote_copy(
            src_ref=src, dst_ref=dst, send_sem=send, recv_sem=recv,
            device_id=target, device_id_type=MESH,
        )

    def wait_bytes(ref, sem):
        pltpu.make_async_copy(ref, ref, sem).wait()

    barrier = pltpu.get_barrier_semaphore()

    @pl.loop(1, n_row)
    def _(i):
        pl.semaphore_signal(
            barrier, inc=1, device_id=(peer(i, row, n_row), col), device_id_type=MESH
        )

    for neighbour in (col_up, col_dn):
        pl.semaphore_signal(barrier, inc=1, device_id=(row, neighbour), device_id_type=MESH)

    loads = [
        pltpu.make_async_copy(src, dst, load.at[i])
        for i, (src, dst) in enumerate(
            (
                (mat_hbm, mat_ref), (vent_hbm, vent_ref),
                (rhs_hbm, rhs_ref), (basis_hbm, basis_ref),
            )
        )
    ]
    for copy in loads:
        copy.start()
    for copy in loads[:2]:
        copy.wait()

    material = mat_ref[...]
    conduct = jnp.zeros(material.shape, F32)
    heat = jnp.zeros(material.shape, F32)
    for class_id in range(con_ref.shape[0]):
        hit = material == class_id
        conduct = jnp.where(hit, con_ref[class_id], conduct)
        heat = jnp.where(hit, cap_ref[class_id], heat)
    vent = vent_ref[...]
    partner = [par_ref[k] for k in range(2)]
    info_row = lax.broadcasted_iota(jnp.int32, (8, LANES), 0)
    info[row] = jnp.where(
        info_row == 0, partner[0].astype(F32), jnp.where(info_row == 1, partner[1].astype(F32), 0.0)
    )
    line_id = lax.broadcasted_iota(jnp.int32, (lines, depth), 0)
    lane_id = lax.broadcasted_iota(jnp.int32, (lines, depth), 1)
    on_first, on_last = lane_id == line_id, lane_id == line_id + lines

    def pack_sides(first, last):
        spread = jnp.where(on_first, first, 0.0) + jnp.where(on_last, last, 0.0)
        return jnp.sum(spread, axis=0, keepdims=True)

    def send_sides(at, packed):
        ysend[at] = jnp.broadcast_to(packed, (8, LANES))
        for copy in y_copies(at):
            copy.start()

    def send_top(at, top):
        tops[at][row] = top
        for other in row_peers():
            remote(
                tops[at].at[row], tops[at].at[row], top_s.at[at], top_r.at[at], (other, col)
            ).start()

    def send_lines(at, values):
        fields[at, :, 8 : 8 + width, :] = values
        for copy in x_copies(at):
            copy.start()

    def start_exchange(at, values, top):
        flat = values.reshape(lines, depth)
        send_sides(at, pack_sides(flat[:, 0:1], flat[:, depth - 1 : depth]))
        send_top(at, top)
        send_lines(at, values)

    def x_copies(at):
        return (
            remote(
                fields.at[at, :, pl.ds(7 + width, 1), :], fields.at[at, :, pl.ds(7, 1), :],
                x_s.at[at, 0], x_r.at[at, 0], (row_up, col),
            ),
            remote(
                fields.at[at, :, pl.ds(8, 1), :], fields.at[at, :, pl.ds(8 + width, 1), :],
                x_s.at[at, 1], x_r.at[at, 1], (row_dn, col),
            ),
        )

    def y_copies(at):
        return (
            remote(ysend.at[at], yrecv.at[at, 0], y_s.at[at, 0], y_r.at[at, 0], (row, col_up)),
            remote(ysend.at[at], yrecv.at[at, 1], y_s.at[at, 1], y_r.at[at, 1], (row, col_dn)),
        )

    def finish_exchange(at, values):
        for copy in x_copies(at):
            copy.wait_recv()
        wait_bytes(tops[at].at[pl.ds(0, n_row - 1)], top_r.at[at])
        for copy in y_copies(at):
            copy.wait_recv()
        flat = values.reshape(lines, depth)
        from_dn = jnp.where(on_last, yrecv[at, 0, 0:1, :], 0.0)
        from_up = jnp.where(on_first, yrecv[at, 1, 0:1, :], 0.0)
        dn_y = jnp.where(
            lane_id == 0, jnp.sum(from_dn, axis=1, keepdims=True), pltpu.roll(flat, 1, 1)
        ).reshape(values.shape)
        up_y = jnp.where(
            lane_id == depth - 1,
            jnp.sum(from_up, axis=1, keepdims=True),
            pltpu.roll(flat, depth - 1, 1),
        ).reshape(values.shape)
        dn_x = fields[at, :, 7 : 7 + width, :]
        up_x = fields[at, :, 9 : 9 + width, :]
        coupled = tops[at][partner[0]] + tops[at][partner[1]]
        return up_x, dn_x, up_y, dn_y, coupled

    pl.semaphore_wait(barrier, n_row - 1 + 2)
    start_exchange(0, conduct, vent)

    @pl.loop(1, n_row)
    def _(i):
        remote(info.at[row], info.at[row], info_s, info_r, (peer(i, row, n_row), col)).start()

    for copy in loads[2:]:
        copy.wait()

    @pl.loop(0, vectors, unroll=4)
    def _(a):
        zf[pl.ds(a * PITCH, lines), :] = basis_ref[a].astype(F32)

    zk[lines * vectors :, :] = jnp.zeros((width * vectors, depth), F32)

    def line(k):
        return pl.ds(k * vectors, vectors)

    basis_lane = lax.broadcasted_iota(jnp.int32, (vectors, depth), 1)

    def turn(k, sides):
        block = zf[pl.ds(k, vectors, stride=PITCH), :]
        zk[line(k), :] = block
        zr[:, pl.ds(pl.multiple_of(k * depth, depth), depth)] = block.astype(BF16)
        sides = jnp.where(basis_lane == k, block[:, 0:1], sides)
        return jnp.where(basis_lane == lines + k, block[:, depth - 1 : depth], sides)

    yb[...] = lax.fori_loop(0, lines, turn, jnp.zeros((vectors, depth), F32), unroll=8)
    ybs[...] = yb[...].astype(BF16)
    side_basis = (
        remote(ybs, ybr.at[0], yb_s.at[0], yb_r.at[0], (row, col_up)),
        remote(ybs, ybr.at[1], yb_s.at[1], yb_r.at[1], (row, col_dn)),
    )

    def cells(k):
        return pl.ds(pl.multiple_of(k * depth, depth), depth)

    def face_copies():
        copies = []
        for z in range(layers):
            there = pl.ds(z * depth, depth)
            copies.append(
                remote(
                    zr.at[:, cells(z * width + width - 1)], xb.at[0, :, there],
                    xb_s.at[0, z], xb_r.at[0, z], (row_up, col),
                )
            )
            copies.append(
                remote(
                    zr.at[:, cells(z * width)], xb.at[1, :, there],
                    xb_s.at[1, z], xb_r.at[1, z], (row_dn, col),
                )
            )
        return copies

    top_line = (layers - 1) * width
    for copy in face_copies() + list(side_basis):
        copy.start()

    @pl.loop(1, n_row)
    def _(i):
        target = peer(i, row, n_row)
        first = top_line + target * share
        remote(
            zr.at[:, pl.ds(pl.multiple_of(first * depth, depth), share * depth)], pa.at[row],
            pa_s, pa_r, (target, col),
        ).start()

    def project(values):
        work[...] = values.reshape(lines, depth)

        def step(k, total):
            return total + zk[line(k), :] * work[pl.ds(k, 1), :]

        total = lax.fori_loop(0, lines, step, jnp.zeros((vectors, depth), F32), unroll=8)
        return jnp.sum(total, axis=1, keepdims=True)

    def expand(at, coarse):
        spread = jnp.broadcast_to(coarse, wide.shape)
        wide[...] = spread
        send_sides(at, jnp.sum(spread * yb[...], axis=0, keepdims=True))

        def part(first, count):
            def step(a, total):
                return total + zf[pl.ds(a * PITCH + first, count), :] * wide[pl.ds(a, 1), :]

            return lax.fori_loop(0, vectors, step, jnp.zeros((count, depth), F32), unroll=8)

        top = part(top_line, width)
        send_top(at, vent * top)
        rest = part(0, top_line)
        total = jnp.concatenate([rest, top], axis=0).reshape(layers, width, depth)
        send_lines(at, total)
        return total

    square_row = lax.broadcasted_iota(jnp.int32, (vectors, vectors), 0)
    square_col = lax.broadcasted_iota(jnp.int32, (vectors, vectors), 1)

    def solve(right_side):
        flat = jnp.sum(jnp.where(square_row == square_col, right_side, 0.0), axis=0, keepdims=True)
        return jnp.sum(inv_ref[...] * flat, axis=1, keepdims=True)

    rhs = rhs_ref[...]
    first_side = project(rhs)

    x_id = lax.broadcasted_iota(jnp.int32, conduct.shape, 1)
    y_id = lax.broadcasted_iota(jnp.int32, conduct.shape, 2)
    x_last, x_first = x_id == width - 1, x_id == 0
    y_last, y_first = y_id == depth - 1, y_id == 0
    none = jnp.zeros((1, width, depth), F32)
    up_z = jnp.concatenate([harmonic(conduct[:-1], conduct[1:]), none], axis=0)
    dn_z = jnp.concatenate([none, up_z[:-1]], axis=0)
    in_up_x = jnp.where(x_last, 0.0, harmonic(conduct, pltpu.roll(conduct, width - 1, 1)))
    in_dn_x = jnp.where(x_first, 0.0, pltpu.roll(in_up_x, 1, 1))
    in_up_y = jnp.where(y_last, 0.0, harmonic(conduct, pltpu.roll(conduct, depth - 1, 2)))
    in_dn_y = jnp.where(y_first, 0.0, pltpu.roll(in_up_y, 1, 2))
    inside = heat + up_z + dn_z + in_up_x + in_dn_x + in_up_y + in_dn_y
    for c, part in enumerate((0.5 * inside, up_z, in_up_x, in_up_y)):
        coef[c] = part.reshape(lines, depth)

    def keep(rows, where):
        high, low = split(rows)
        az[0:vectors, where] = high
        az[vectors : 2 * vectors, where] = low

    @pl.loop(0, lines, unroll=4)
    def _(k):
        own = zk[line(k), :]

        def at(c):
            return coef[c, pl.ds(k, 1), :]

        applied = at(0) * own - at(1) * zk[line(k + width), :]
        applied = applied - at(2) * zk[line(k + 1), :] - at(3) * pltpu.roll(own, depth - 1, 1)
        keep(applied, cells(k))

    half = dot_t(az[...], zr[...])
    half = half[:vectors] + half[vectors:]
    own_block = half + half.T

    near = finish_exchange(0, conduct)
    out_up_x = jnp.where(x_last & (row < n_row - 1), harmonic(conduct, near[0]), 0.0)
    out_dn_x = jnp.where(x_first & (row > 0), harmonic(conduct, near[1]), 0.0)
    out_up_y = jnp.where(y_last & (col < n_col - 1), harmonic(conduct, near[2]), 0.0)
    out_dn_y = jnp.where(y_first & (col > 0), harmonic(conduct, near[3]), 0.0)
    up_x, dn_x = in_up_x + out_up_x, in_dn_x + out_dn_x
    up_y, dn_y = in_up_y + out_up_y, in_dn_y + out_dn_y
    outside = jnp.concatenate(
        [(out_up_x + out_dn_x)[:-1], (out_up_x + out_dn_x)[-1:] + (vent * near[4])[None]], axis=0
    )
    diagonal = inside + outside + out_up_y + out_dn_y

    outer = [z * width + x for z in range(layers - 1) for x in (0, width - 1)]
    outer += list(range(top_line, lines))
    coef[4] = outside.reshape(lines, depth)
    for i, k in enumerate(outer):
        there = pl.ds(i * depth, depth)
        keep(coef[4, k : k + 1, :] * zk[line(k), :], there)
        zo[:, there] = zr[:, cells(k)]
    side_gain = pack_sides(
        out_dn_y.reshape(lines, depth)[:, 0:1], out_up_y.reshape(lines, depth)[:, depth - 1 : depth]
    )
    there = pl.ds(len(outer) * depth, depth)
    keep(side_gain * yb[...], there)
    zo[:, there] = yb[...].astype(BF16)
    size = (len(outer) + 1) * depth
    extra = dot_t(az[:, :size], zo[...])
    own_block = own_block + extra[:vectors] + extra[vectors:]
    inv_ref[...] = inverse(own_block)

    def apply_start(at, values):
        start_exchange(at, values, vent * values[layers - 1])

    def apply_finish(at, values):
        near = finish_exchange(at, values)
        none = jnp.zeros((1, width, depth), F32)
        result = diagonal * values
        result = result - up_z * jnp.concatenate([values[1:], none], axis=0)
        result = result - dn_z * jnp.concatenate([none, values[:-1]], axis=0)
        result = result - up_x * near[0] - dn_x * near[1] - up_y * near[2] - dn_y * near[3]
        return jnp.concatenate([result[:-1], (result[-1] - vent * near[4])[None]], axis=0)

    def apply(at, values, beside):
        apply_start(at, values)
        beside()
        return apply_finish(at, values)

    def apply_coarse(at, coarse, beside):
        values = expand(at, coarse)
        beside()
        return values, apply_finish(at, values)

    def correct(at, right_side, besides):
        first, first_image = apply_coarse(at, solve(right_side), besides[0])
        second, second_image = apply_coarse(
            at + 1, solve(right_side - project(first_image)), besides[1]
        )
        return first + second, first_image + second_image

    def coarse_copies(at):
        i = COARSE_ROUNDS.index(at)
        return (
            remote(ysv.at[i], yrv.at[i, 0], y_s.at[at, 0], y_r.at[at, 0], (row, col_up)),
            remote(ysv.at[i], yrv.at[i, 1], y_s.at[at, 1], y_r.at[at, 1], (row, col_dn)),
        )

    def correct_by_blocks(at, right_side, besides):
        coarse = solve(right_side)
        i, held = COARSE_ROUNDS.index(at), coarse_rows[at]
        packed = jnp.broadcast_to(pack_sides(coarse, coarse), (8, LANES))
        ysv[i] = packed
        held[row] = packed
        for copy in coarse_copies(at):
            copy.start()
        mine = held.at[row, pl.ds(0, 1)]
        for other in row_peers():
            remote(mine, mine, top_s.at[at], top_r.at[at], (other, col)).start()
        besides[0]()
        for copy in coarse_copies(at):
            copy.wait_recv()
        wait_bytes(held.at[pl.ds(0, n_row - 1), pl.ds(0, 1)], top_r.at[at])
        first_half = lax.broadcasted_iota(jnp.int32, (1, LANES), 1) < vectors
        pairs = (
            (held[row_dn, 0:1], held[row_up, 0:1]),
            (yrv[i, 0, 0:1], yrv[i, 1, 0:1]),
            (held[partner[0], 0:1], held[partner[1], 0:1]),
        )
        total = jnp.zeros((vectors, 2 * vectors), F32)
        for pair, (left, right) in enumerate(pairs):
            total = total + eb[pair] * jnp.where(first_half, left, right)
        coarse = coarse - solve(jnp.sum(total, axis=1, keepdims=True))
        return apply_coarse(at + 1, coarse, besides[1])

    def faces():
        for copy in face_copies() + list(side_basis):
            copy.wait_recv()
        halves = [pltpu.roll(ybr[side].astype(F32), depth - lines, 1) for side in range(2)]
        high, low = split(side_gain * yb[...])
        both = dot_t(
            jnp.concatenate([high, low], axis=0),
            jnp.concatenate(
                [
                    jnp.where(basis_lane < lines, halves[0], 0.0),
                    jnp.where(basis_lane < lines, 0.0, halves[1]),
                ],
                axis=0,
            ).astype(BF16),
        )
        eb[1] = -(both[:vectors] + both[vectors:])
        for side, at, coefficient in ((0, 0, dn_x), (1, width - 1, up_x)):
            terms = [
                zk[line(z * width + at), :] * coefficient[z, at : at + 1, :] for z in range(layers)
            ]
            high, low = split(jnp.concatenate(terms, axis=1))
            both = dot_t(jnp.concatenate([high, low], axis=0), xb[side])
            wide_faces[side] = both[:vectors] + both[vectors:]

    wide_faces = [None, None]

    def couplings():
        eb[0] = -jnp.concatenate(wide_faces, axis=1)
        wait_bytes(pc.at[pl.ds(0, n_row - 1)], pc_r)
        eb[2] = -lax.fori_loop(
            0, n_row, lambda i, t: t + pc[i], jnp.zeros((vectors, 2 * vectors), F32)
        )

    third = n_row // 3

    def nothing():
        pass

    def begin():
        faces()
        plenum_start()
        plenum(0, third)

    def plenum_start():
        wait_bytes(info.at[pl.ds(0, n_row - 1)], info_r)
        wait_bytes(pa.at[pl.ds(0, n_row - 1)], pa_r)
        first = top_line + row * share
        pa[row] = zr[:, pl.ds(pl.multiple_of(first * depth, depth), share * depth)]

    def plenum(first, last):
        @pl.loop(first, last)
        def _(offset):
            s = peer(offset, row, n_row)
            own = pa[s]
            total = None
            for i in range(share):
                rows = []
                for k in range(2):
                    which = info[s, k : k + 1, :]
                    chosen = jnp.zeros((vectors, depth), F32)
                    gain = jnp.zeros((1, depth), F32)
                    for t in range(n_row):
                        block = pa[t, :, i * depth : (i + 1) * depth].astype(F32)
                        gain = jnp.where(which == t, tops[0][t, pl.ds(row * share + i, 1), :], gain)
                        chosen = jnp.where(which == t, block, chosen)
                    rows.append(chosen * (gain * tops[0][s, pl.ds(row * share + i, 1), :]))
                high, low = split(jnp.concatenate(rows, axis=0))
                mine = own[:, i * depth : (i + 1) * depth]
                part = dot_t(
                    jnp.concatenate([mine, mine], axis=1), jnp.concatenate([high, low], axis=1)
                )
                total = part if total is None else total + part
            pb[s] = total

            @pl.when(offset > 0)
            def _():
                remote(pb.at[s], pc.at[row], pc_s, pc_r, (s, col)).start()

            @pl.when(offset == 0)
            def _():
                pc[row] = pb[s]

    def finish_blocks():
        scale = 1.0 / (lines * depth)
        parts = (
            own_block * scale, eb[0, :, :vectors] * scale, eb[0, :, vectors:] * scale,
            eb[2, :, :vectors] * scale, eb[2, :, vectors:] * scale,
        )

        @pl.loop(0, n_row)
        def _(q):
            hits = (q == row, q == row - 1, q == row + 1, q == partner[0], q == partner[1])
            value = jnp.zeros((vectors, vectors), F32)
            for hit, part in zip(hits, parts):
                value = value + jnp.where(hit, 1.0, 0.0) * part
            e_ref[q] = value

    iterate, image = correct(
        1, first_side, (begin, lambda: plenum(third, 2 * third))
    )
    defect = rhs - image
    turned = apply(3, defect, lambda: plenum(2 * third, n_row))
    shift, image = correct_by_blocks(4, project(turned), (couplings, nothing))
    direction, stepped = defect - shift, turned - image
    turned = apply(6, stepped, finish_blocks)
    shift, image = correct_by_blocks(7, project(turned), (nothing, nothing))
    slanted, slanted_image = stepped - shift, turned - image

    def lanes_of(left, right):
        return jnp.sum((left * right).reshape(lines, depth), axis=0, keepdims=True)

    sums = [
        lanes_of(defect, defect), lanes_of(direction, stepped), lanes_of(defect, stepped),
        lanes_of(stepped, stepped), lanes_of(slanted, stepped), lanes_of(slanted, slanted_image),
    ]
    sums = jnp.concatenate(sums + [jnp.zeros((2, depth), F32)], axis=0)
    scalar_at = lax.broadcasted_iota(jnp.int32, (8, LANES), 0) == lax.broadcasted_iota(
        jnp.int32, (8, LANES), 1
    )
    sums = jnp.where(scalar_at, jnp.sum(sums, axis=1, keepdims=True), 0.0)
    red_row[row] = jnp.sum(sums, axis=0, keepdims=True)
    for other in row_peers():
        remote(red_row.at[row], red_row.at[row], rr_s, rr_r, (other, col)).start()
    wait_bytes(red_row.at[pl.ds(0, n_row - 1)], rr_r)
    red_col[col] = jnp.sum(red_row[...], axis=0)
    ring = n_col // 2
    for i in sorted(range(1, n_col), key=lambda i: min(i % ring, ring - i % ring), reverse=True):
        remote(red_col.at[col], red_col.at[col], rc_s, rc_r, (row, peer(i, col, n_col))).start()
    wait_bytes(red_col.at[pl.ds(0, n_col - 1)], rc_r)
    scalars = jnp.where(scalar_at, jnp.sum(red_col[...], axis=0), 0.0)
    scalars = jnp.sum(scalars, axis=1, keepdims=True)
    norm, curve, cross, square, mixed, slant = [scalars[i : i + 1, :] for i in range(6)]
    alpha = norm / curve
    after = norm - 2.0 * alpha * cross + alpha * alpha * square
    gain = 1.0 + after / norm
    curve = gain * gain * curve - 2.0 * gain * alpha * mixed + alpha * alpha * slant
    last = after / curve

    def scaled(factor, values):
        return jnp.broadcast_to(factor, values.shape) * values

    alpha, gain, last = alpha[None], gain[None], last[None]
    x_ref[...] = (
        iterate
        + scaled(alpha, direction)
        + scaled(last, scaled(gain, direction) - scaled(alpha, slanted))
    )
    r_ref[...] = (
        defect
        - scaled(alpha, stepped)
        - scaled(last, scaled(gain, stepped) - scaled(alpha, slanted_image))
    )

    for at in range(ROUNDS):
        if at in COARSE_ROUNDS:
            for copy in coarse_copies(at):
                copy.wait_send()
            wait_bytes(coarse_rows[at].at[pl.ds(0, n_row - 1), pl.ds(0, 1)], top_s.at[at])
        else:
            for copy in x_copies(at) + y_copies(at):
                copy.wait_send()
            wait_bytes(tops[at].at[pl.ds(0, n_row - 1)], top_s.at[at])

    for copy in face_copies() + list(side_basis):
        copy.wait_send()
    wait_bytes(info.at[pl.ds(0, n_row - 1)], info_s)
    wait_bytes(pa.at[pl.ds(0, n_row - 1)], pa_s)
    wait_bytes(pc.at[pl.ds(0, n_row - 1)], pc_s)
    wait_bytes(red_row.at[pl.ds(0, n_row - 1)], rr_s)
    wait_bytes(red_col.at[pl.ds(0, n_col - 1)], rc_s)


def body(n_row, n_col, rhs, material, capacity, conductivity, vent, partners, basis):
    layers, width, depth = rhs.shape
    vectors = basis.shape[0]
    lines, share = layers * width, width // n_row
    smem, vmem = pl.BlockSpec(memory_space=pltpu.SMEM), pl.BlockSpec(memory_space=pltpu.VMEM)
    hbm = pl.BlockSpec(memory_space=pltpu.HBM)
    outer = 2 * (layers - 1) + width
    dma = pltpu.SemaphoreType.DMA
    scratch = [
        pltpu.VMEM(rhs.shape, F32), pltpu.VMEM(material.shape, jnp.int32),
        pltpu.VMEM(vent.shape, F32), pltpu.VMEM((vectors, lines, depth), BF16),
        pltpu.VMEM((ROUNDS, layers, width + 16, depth), F32),
        pltpu.VMEM((ROUNDS, 8, LANES), F32),
        pltpu.VMEM((ROUNDS, 2, 8, LANES), F32),
        pltpu.VMEM((n_row, 8, LANES), F32),
        pltpu.VMEM((vectors * PITCH, depth), F32),
        pltpu.VMEM((vectors * (lines + width), depth), F32),
        pltpu.VMEM((vectors, lines * depth), BF16),
        pltpu.VMEM((vectors, depth), F32),
        pltpu.VMEM((vectors, depth), BF16),
        pltpu.VMEM((2, vectors, depth), BF16),
        pltpu.VMEM((3, vectors, 2 * vectors), F32),
        pltpu.VMEM((len(COARSE_ROUNDS), 8, LANES), F32),
        pltpu.VMEM((len(COARSE_ROUNDS), 2, 8, LANES), F32),
        pltpu.VMEM((2 * vectors, lines * depth), BF16),
        pltpu.VMEM((2, vectors, layers * depth), BF16),
        pltpu.VMEM((n_row, vectors, share * depth), BF16),
        pltpu.VMEM((n_row, vectors, 2 * vectors), F32),
        pltpu.VMEM((n_row, vectors, 2 * vectors), F32),
        pltpu.VMEM((5, lines, depth), F32),
        pltpu.VMEM((vectors, (outer + 1) * depth), BF16),
        pltpu.VMEM((lines, depth), F32),
        pltpu.VMEM((vectors, depth), F32),
        pltpu.VMEM((vectors, vectors), F32),
        pltpu.VMEM((n_row, 1, LANES), F32),
        pltpu.VMEM((n_col, 1, LANES), F32),
        dma((4,)), dma((ROUNDS,)), dma((ROUNDS,)), dma((ROUNDS, 2)), dma((ROUNDS, 2)),
        dma((ROUNDS, 2)), dma((ROUNDS, 2)), dma, dma, dma((2,)), dma((2,)), dma((2, layers)), dma((2, layers)),
        dma, dma, dma, dma, dma, dma, dma, dma,
        *[pltpu.VMEM((n_row, width, depth), F32) for _ in range(ROUNDS)],
        *[pltpu.VMEM((n_row, 8, LANES), F32) for _ in COARSE_ROUNDS],
    ]
    iterate, defect, blocks = pl.pallas_call(
        functools.partial(kernel, n_row, n_col),
        out_shape=(
            jax.ShapeDtypeStruct(rhs.shape, F32),
            jax.ShapeDtypeStruct(rhs.shape, F32),
            jax.ShapeDtypeStruct((n_row, vectors, vectors), F32),
        ),
        in_specs=[smem, smem, smem, hbm, hbm, hbm, hbm],
        out_specs=(vmem, vmem, vmem),
        scratch_shapes=scratch,
        compiler_params=pltpu.CompilerParams(
            collective_id=0, has_side_effects=True, vmem_limit_bytes=67043328
        ),
        name="deflated_cg",
    )(
        capacity, conductivity, partners.reshape(-1), rhs, material, vent,
        basis.reshape(vectors, lines, depth),
    )
    return iterate, defect, blocks[None, None]


def solution(mesh):
    n_row, n_col = mesh.shape["row"], mesh.shape["col"]
    return jax.shard_map(
        functools.partial(body, n_row, n_col),
        mesh=mesh,
        in_specs=(
            P(None, "row", "col"),
            P(None, "row", "col"),
            P(),
            P(),
            P("row", "col"),
            P("row", "col", None),
            P(None, None, "row", "col"),
        ),
        out_specs=(P(None, "row", "col"), P(None, "row", "col"), P("row", "col", None, None, None)),
        check_vma=False,
    )
```

```python
import functools

import jax
import jax.numpy as jnp
from jax import lax
from jax.experimental import pallas as pl
from jax.experimental.pallas import tpu as pltpu
from jax.sharding import PartitionSpec as P

MESH = pl.DeviceIdType.MESH
F32, BF16 = jnp.float32, jnp.bfloat16
LANES = 128
PIVOTS = 4
ROUNDS = 9
PITCH = 72
COARSE_ROUNDS = (7,)


def harmonic(left_side, right_side):
    return 2.0 * left_side * right_side / (left_side + right_side)


def split(values):
    high = values.astype(BF16)
    return high, (values - high.astype(F32)).astype(BF16)


def dot_t(left, right):
    return lax.dot_general(left, right, (((1,), (1,)), ((), ())), preferred_element_type=F32)


def inverse(matrix):
    n = matrix.shape[0]
    row_id = lax.broadcasted_iota(jnp.int32, (n, n), 0)
    col_id = lax.broadcasted_iota(jnp.int32, (n, n), 1)
    work = jnp.concatenate([matrix, (row_id == col_id).astype(F32)], axis=1)
    wide_row = lax.broadcasted_iota(jnp.int32, work.shape, 0)
    for base in range(0, n, PIVOTS):
        ids = range(PIVOTS)
        rows = [work[base + i : base + i + 1, :] for i in ids]
        pivot = [
            [jnp.broadcast_to(rows[i][:, base + j : base + j + 1], rows[i].shape) for j in ids]
            for i in ids
        ]
        inside = (wide_row >= base) & (wide_row < base + PIVOTS)
        columns = [
            jnp.where(
                inside,
                jnp.where(wide_row == base + j, -1.0, 0.0),
                jnp.broadcast_to(work[:, base + j : base + j + 1], work.shape),
            )
            for j in ids
        ]
        work = jnp.where(inside, 0.0, work)
        for p in range(0, PIVOTS, 2):
            (a, b), (c, d) = (pivot[p + i][p : p + 2] for i in range(2))
            scale = 1.0 / (a * d - b * c)
            a, b, c, d = d * scale, -b * scale, -c * scale, a * scale
            rows[p], rows[p + 1] = a * rows[p] + b * rows[p + 1], c * rows[p] + d * rows[p + 1]
            for j in range(p + 2, PIVOTS):
                first, second = pivot[p][j], pivot[p + 1][j]
                pivot[p][j], pivot[p + 1][j] = a * first + b * second, c * first + d * second
            for i in ids:
                if i not in (p, p + 1):
                    first, second = pivot[i][p], pivot[i][p + 1]
                    rows[i] = rows[i] - (first * rows[p] + second * rows[p + 1])
                    for j in range(p + 2, PIVOTS):
                        pivot[i][j] = pivot[i][j] - (
                            first * pivot[p][j] + second * pivot[p + 1][j]
                        )
        for j in ids:
            work = work - columns[j] * rows[j]
    return work[:, n:]


def kernel(
    n_row, n_col,
    cap_ref, con_ref, par_ref, rhs_hbm, mat_hbm, vent_hbm, basis_hbm,
    x_ref, r_ref, e_ref,
    rhs_ref, mat_ref, vent_ref, basis_ref,
    fields, ysend, yrecv, info, zf, zk, zr, yb, ybs, ybr, eb, ysv, yrv, az, xb, pa, pb, pc, coef, zo, work, wide, inv_ref,
    red_row, red_col, load,
    top_s, top_r, x_s, x_r, y_s, y_r, info_s, info_r, yb_s, yb_r, xb_s, xb_r, pa_s, pa_r, pc_s, pc_r,
    rr_s, rr_r, rc_s, rc_r, *more,
):
    tops, coarse_rows = more[:ROUNDS], dict(zip(COARSE_ROUNDS, more[ROUNDS:]))
    layers, width, depth = rhs_ref.shape
    vectors = basis_ref.shape[0]
    lines = layers * width
    share = width // n_row
    row, col = lax.axis_index("row"), lax.axis_index("col")
    row_up, row_dn = lax.rem(row + 1, n_row), lax.rem(row + n_row - 1, n_row)
    col_up, col_dn = lax.rem(col + 1, n_col), lax.rem(col + n_col - 1, n_col)

    count_x = n_row // 4
    steps = [(dx, dy, dc) for dx in range(count_x) for dy in range(2) for dc in range(2)]
    steps = sorted(steps[1:], key=lambda s: (min(s[0], count_x - s[0]) + s[1], s), reverse=True)

    def peer(i, me, count):
        return lax.rem(me + i, count)

    def row_peers():
        x, rest = row // 4, lax.rem(row, 4)
        for dx, dy, dc in steps:
            yield (
                lax.rem(x + dx, count_x) * 4
                + lax.rem(rest // 2 + dy, 2) * 2
                + lax.rem(lax.rem(rest, 2) + dc, 2)
            )

    def remote(src, dst, send, recv, target):
        return pltpu.make_async_remote_copy(
            src_ref=src, dst_ref=dst, send_sem=send, recv_sem=recv,
            device_id=target, device_id_type=MESH,
        )

    def wait_bytes(ref, sem):
        pltpu.make_async_copy(ref, ref, sem).wait()

    barrier = pltpu.get_barrier_semaphore()

    @pl.loop(1, n_row)
    def _(i):
        pl.semaphore_signal(
            barrier, inc=1, device_id=(peer(i, row, n_row), col), device_id_type=MESH
        )

    for neighbour in (col_up, col_dn):
        pl.semaphore_signal(barrier, inc=1, device_id=(row, neighbour), device_id_type=MESH)

    loads = [
        pltpu.make_async_copy(src, dst, load.at[i])
        for i, (src, dst) in enumerate(
            (
                (mat_hbm, mat_ref), (vent_hbm, vent_ref),
                (rhs_hbm, rhs_ref), (basis_hbm, basis_ref),
            )
        )
    ]
    for copy in loads:
        copy.start()
    for copy in loads[:2]:
        copy.wait()

    material = mat_ref[...]
    conduct = jnp.zeros(material.shape, F32)
    heat = jnp.zeros(material.shape, F32)
    for class_id in range(con_ref.shape[0]):
        hit = material == class_id
        conduct = jnp.where(hit, con_ref[class_id], conduct)
        heat = jnp.where(hit, cap_ref[class_id], heat)
    vent = vent_ref[...]
    partner = [par_ref[k] for k in range(2)]
    info_row = lax.broadcasted_iota(jnp.int32, (8, LANES), 0)
    info[row] = jnp.where(
        info_row == 0, partner[0].astype(F32), jnp.where(info_row == 1, partner[1].astype(F32), 0.0)
    )
    line_id = lax.broadcasted_iota(jnp.int32, (lines, depth), 0)
    lane_id = lax.broadcasted_iota(jnp.int32, (lines, depth), 1)
    on_first, on_last = lane_id == line_id, lane_id == line_id + lines

    def pack_sides(first, last):
        spread = jnp.where(on_first, first, 0.0) + jnp.where(on_last, last, 0.0)
        return jnp.sum(spread, axis=0, keepdims=True)

    def send_sides(at, packed):
        ysend[at] = jnp.broadcast_to(packed, (8, LANES))
        for copy in y_copies(at):
            copy.start()

    def send_top(at, top):
        tops[at][row] = top
        for other in row_peers():
            remote(
                tops[at].at[row], tops[at].at[row], top_s.at[at], top_r.at[at], (other, col)
            ).start()

    def send_lines(at, values):
        fields[at, :, 8 : 8 + width, :] = values
        for copy in x_copies(at):
            copy.start()

    def start_exchange(at, values, top):
        flat = values.reshape(lines, depth)
        send_top(at, top)
        send_sides(at, pack_sides(flat[:, 0:1], flat[:, depth - 1 : depth]))
        send_lines(at, values)

    def x_copies(at):
        return (
            remote(
                fields.at[at, :, pl.ds(7 + width, 1), :], fields.at[at, :, pl.ds(7, 1), :],
                x_s.at[at, 0], x_r.at[at, 0], (row_up, col),
            ),
            remote(
                fields.at[at, :, pl.ds(8, 1), :], fields.at[at, :, pl.ds(8 + width, 1), :],
                x_s.at[at, 1], x_r.at[at, 1], (row_dn, col),
            ),
        )

    def y_copies(at):
        return (
            remote(ysend.at[at], yrecv.at[at, 0], y_s.at[at, 0], y_r.at[at, 0], (row, col_up)),
            remote(ysend.at[at], yrecv.at[at, 1], y_s.at[at, 1], y_r.at[at, 1], (row, col_dn)),
        )

    def finish_exchange(at, values):
        for copy in x_copies(at):
            copy.wait_recv()
        wait_bytes(tops[at].at[pl.ds(0, n_row - 1)], top_r.at[at])
        for copy in y_copies(at):
            copy.wait_recv()
        flat = values.reshape(lines, depth)
        from_dn = jnp.where(on_last, yrecv[at, 0, 0:1, :], 0.0)
        from_up = jnp.where(on_first, yrecv[at, 1, 0:1, :], 0.0)
        dn_y = jnp.where(
            lane_id == 0, jnp.sum(from_dn, axis=1, keepdims=True), pltpu.roll(flat, 1, 1)
        ).reshape(values.shape)
        up_y = jnp.where(
            lane_id == depth - 1,
            jnp.sum(from_up, axis=1, keepdims=True),
            pltpu.roll(flat, depth - 1, 1),
        ).reshape(values.shape)
        dn_x = fields[at, :, 7 : 7 + width, :]
        up_x = fields[at, :, 9 : 9 + width, :]
        coupled = tops[at][partner[0]] + tops[at][partner[1]]
        return up_x, dn_x, up_y, dn_y, coupled

    pl.semaphore_wait(barrier, n_row - 1 + 2)
    start_exchange(0, conduct, vent)

    @pl.loop(1, n_row)
    def _(i):
        remote(info.at[row], info.at[row], info_s, info_r, (peer(i, row, n_row), col)).start()

    for copy in loads[2:]:
        copy.wait()

    @pl.loop(0, vectors, unroll=4)
    def _(a):
        zf[pl.ds(a * PITCH, lines), :] = basis_ref[a].astype(F32)

    zk[lines * vectors :, :] = jnp.zeros((width * vectors, depth), F32)

    def line(k):
        return pl.ds(k * vectors, vectors)

    basis_lane = lax.broadcasted_iota(jnp.int32, (vectors, depth), 1)

    def turn(k, sides):
        block = zf[pl.ds(k, vectors, stride=PITCH), :]
        zk[line(k), :] = block
        zr[:, pl.ds(pl.multiple_of(k * depth, depth), depth)] = block.astype(BF16)
        sides = jnp.where(basis_lane == k, block[:, 0:1], sides)
        return jnp.where(basis_lane == lines + k, block[:, depth - 1 : depth], sides)

    yb[...] = lax.fori_loop(0, lines, turn, jnp.zeros((vectors, depth), F32), unroll=8)
    ybs[...] = yb[...].astype(BF16)
    side_basis = (
        remote(ybs, ybr.at[0], yb_s.at[0], yb_r.at[0], (row, col_up)),
        remote(ybs, ybr.at[1], yb_s.at[1], yb_r.at[1], (row, col_dn)),
    )

    def cells(k):
        return pl.ds(pl.multiple_of(k * depth, depth), depth)

    def face_copies():
        copies = []
        for z in range(layers):
            there = pl.ds(z * depth, depth)
            copies.append(
                remote(
                    zr.at[:, cells(z * width + width - 1)], xb.at[0, :, there],
                    xb_s.at[0, z], xb_r.at[0, z], (row_up, col),
                )
            )
            copies.append(
                remote(
                    zr.at[:, cells(z * width)], xb.at[1, :, there],
                    xb_s.at[1, z], xb_r.at[1, z], (row_dn, col),
                )
            )
        return copies

    top_line = (layers - 1) * width
    for copy in face_copies() + list(side_basis):
        copy.start()

    @pl.loop(1, n_row)
    def _(i):
        target = peer(i, row, n_row)
        first = top_line + target * share
        remote(
            zr.at[:, pl.ds(pl.multiple_of(first * depth, depth), share * depth)], pa.at[row],
            pa_s, pa_r, (target, col),
        ).start()

    def project(values):
        work[...] = values.reshape(lines, depth)

        def step(k, total):
            return total + zk[line(k), :] * work[pl.ds(k, 1), :]

        total = lax.fori_loop(0, lines, step, jnp.zeros((vectors, depth), F32), unroll=32)
        return jnp.sum(total, axis=1, keepdims=True)

    def expand(at, coarse):
        spread = jnp.broadcast_to(coarse, wide.shape)
        wide[...] = spread
        send_sides(at, jnp.sum(spread * yb[...], axis=0, keepdims=True))

        def part(first, count):
            def step(a, total):
                return total + zf[pl.ds(a * PITCH + first, count), :] * wide[pl.ds(a, 1), :]

            return lax.fori_loop(0, vectors, step, jnp.zeros((count, depth), F32), unroll=32)

        top = part(top_line, width)
        send_top(at, vent * top)
        rest = part(0, top_line)
        total = jnp.concatenate([rest, top], axis=0).reshape(layers, width, depth)
        send_lines(at, total)
        return total

    square_row = lax.broadcasted_iota(jnp.int32, (vectors, vectors), 0)
    square_col = lax.broadcasted_iota(jnp.int32, (vectors, vectors), 1)

    def solve(right_side):
        flat = jnp.sum(jnp.where(square_row == square_col, right_side, 0.0), axis=0, keepdims=True)
        return jnp.sum(inv_ref[...] * flat, axis=1, keepdims=True)

    rhs = rhs_ref[...]
    first_side = project(rhs)

    x_id = lax.broadcasted_iota(jnp.int32, conduct.shape, 1)
    y_id = lax.broadcasted_iota(jnp.int32, conduct.shape, 2)
    x_last, x_first = x_id == width - 1, x_id == 0
    y_last, y_first = y_id == depth - 1, y_id == 0
    none = jnp.zeros((1, width, depth), F32)
    up_z = jnp.concatenate([harmonic(conduct[:-1], conduct[1:]), none], axis=0)
    dn_z = jnp.concatenate([none, up_z[:-1]], axis=0)
    in_up_x = jnp.where(x_last, 0.0, harmonic(conduct, pltpu.roll(conduct, width - 1, 1)))
    in_dn_x = jnp.where(x_first, 0.0, pltpu.roll(in_up_x, 1, 1))
    in_up_y = jnp.where(y_last, 0.0, harmonic(conduct, pltpu.roll(conduct, depth - 1, 2)))
    in_dn_y = jnp.where(y_first, 0.0, pltpu.roll(in_up_y, 1, 2))
    inside = heat + up_z + dn_z + in_up_x + in_dn_x + in_up_y + in_dn_y
    for c, part in enumerate((0.5 * inside, up_z, in_up_x, in_up_y)):
        coef[c] = part.reshape(lines, depth)

    def keep(rows, where):
        high, low = split(rows)
        az[0:vectors, where] = high
        az[vectors : 2 * vectors, where] = low

    @pl.loop(0, lines, unroll=4)
    def _(k):
        own = zk[line(k), :]

        def at(c):
            return coef[c, pl.ds(k, 1), :]

        applied = at(0) * own - at(1) * zk[line(k + width), :]
        applied = applied - at(2) * zk[line(k + 1), :] - at(3) * pltpu.roll(own, depth - 1, 1)
        keep(applied, cells(k))

    half = dot_t(az[...], zr[...])
    half = half[:vectors] + half[vectors:]
    own_block = half + half.T

    near = finish_exchange(0, conduct)
    out_up_x = jnp.where(x_last & (row < n_row - 1), harmonic(conduct, near[0]), 0.0)
    out_dn_x = jnp.where(x_first & (row > 0), harmonic(conduct, near[1]), 0.0)
    out_up_y = jnp.where(y_last & (col < n_col - 1), harmonic(conduct, near[2]), 0.0)
    out_dn_y = jnp.where(y_first & (col > 0), harmonic(conduct, near[3]), 0.0)
    up_x, dn_x = in_up_x + out_up_x, in_dn_x + out_dn_x
    up_y, dn_y = in_up_y + out_up_y, in_dn_y + out_dn_y
    outside = jnp.concatenate(
        [(out_up_x + out_dn_x)[:-1], (out_up_x + out_dn_x)[-1:] + (vent * near[4])[None]], axis=0
    )
    diagonal = inside + outside + out_up_y + out_dn_y

    outer = [z * width + x for z in range(layers - 1) for x in (0, width - 1)]
    outer += list(range(top_line, lines))
    coef[4] = outside.reshape(lines, depth)
    for i, k in enumerate(outer):
        there = pl.ds(i * depth, depth)
        keep(coef[4, k : k + 1, :] * zk[line(k), :], there)
        zo[:, there] = zr[:, cells(k)]
    side_gain = pack_sides(
        out_dn_y.reshape(lines, depth)[:, 0:1], out_up_y.reshape(lines, depth)[:, depth - 1 : depth]
    )
    there = pl.ds(len(outer) * depth, depth)
    keep(side_gain * yb[...], there)
    zo[:, there] = yb[...].astype(BF16)
    size = (len(outer) + 1) * depth
    extra = dot_t(az[:, :size], zo[...])
    own_block = own_block + extra[:vectors] + extra[vectors:]
    inv_ref[...] = inverse(own_block)

    def apply_start(at, values):
        start_exchange(at, values, vent * values[layers - 1])

    def apply_finish(at, values):
        near = finish_exchange(at, values)
        none = jnp.zeros((1, width, depth), F32)
        result = diagonal * values
        result = result - up_z * jnp.concatenate([values[1:], none], axis=0)
        result = result - dn_z * jnp.concatenate([none, values[:-1]], axis=0)
        result = result - up_x * near[0] - dn_x * near[1] - up_y * near[2] - dn_y * near[3]
        return jnp.concatenate([result[:-1], (result[-1] - vent * near[4])[None]], axis=0)

    def apply(at, values, beside):
        apply_start(at, values)
        beside()
        return apply_finish(at, values)

    def apply_coarse(at, coarse, beside):
        values = expand(at, coarse)
        beside()
        return values, apply_finish(at, values)

    def correct(at, right_side, besides):
        first, first_image = apply_coarse(at, solve(right_side), besides[0])
        second, second_image = apply_coarse(
            at + 1, solve(right_side - project(first_image)), besides[1]
        )
        return first + second, first_image + second_image

    def coarse_copies(at):
        i = COARSE_ROUNDS.index(at)
        return (
            remote(ysv.at[i], yrv.at[i, 0], y_s.at[at, 0], y_r.at[at, 0], (row, col_up)),
            remote(ysv.at[i], yrv.at[i, 1], y_s.at[at, 1], y_r.at[at, 1], (row, col_dn)),
        )

    def correct_by_blocks(at, right_side, besides):
        coarse = solve(right_side)
        i, held = COARSE_ROUNDS.index(at), coarse_rows[at]
        packed = jnp.broadcast_to(pack_sides(coarse, coarse), (8, LANES))
        ysv[i] = packed
        held[row] = packed
        for copy in coarse_copies(at):
            copy.start()
        mine = held.at[row, pl.ds(0, 1)]
        for other in row_peers():
            remote(mine, mine, top_s.at[at], top_r.at[at], (other, col)).start()
        besides[0]()
        for copy in coarse_copies(at):
            copy.wait_recv()
        wait_bytes(held.at[pl.ds(0, n_row - 1), pl.ds(0, 1)], top_r.at[at])
        first_half = lax.broadcasted_iota(jnp.int32, (1, LANES), 1) < vectors
        pairs = (
            (held[row_dn, 0:1], held[row_up, 0:1]),
            (yrv[i, 0, 0:1], yrv[i, 1, 0:1]),
            (held[partner[0], 0:1], held[partner[1], 0:1]),
        )
        total = jnp.zeros((vectors, 2 * vectors), F32)
        for pair, (left, right) in enumerate(pairs):
            total = total + eb[pair] * jnp.where(first_half, left, right)
        coarse = coarse - solve(jnp.sum(total, axis=1, keepdims=True))
        return apply_coarse(at + 1, coarse, besides[1])

    def faces():
        for copy in face_copies() + list(side_basis):
            copy.wait_recv()
        halves = [pltpu.roll(ybr[side].astype(F32), depth - lines, 1) for side in range(2)]
        high, low = split(side_gain * yb[...])
        both = dot_t(
            jnp.concatenate([high, low], axis=0),
            jnp.concatenate(
                [
                    jnp.where(basis_lane < lines, halves[0], 0.0),
                    jnp.where(basis_lane < lines, 0.0, halves[1]),
                ],
                axis=0,
            ).astype(BF16),
        )
        eb[1] = -(both[:vectors] + both[vectors:])
        for side, at, coefficient in ((0, 0, dn_x), (1, width - 1, up_x)):
            terms = [
                zk[line(z * width + at), :] * coefficient[z, at : at + 1, :] for z in range(layers)
            ]
            high, low = split(jnp.concatenate(terms, axis=1))
            both = dot_t(jnp.concatenate([high, low], axis=0), xb[side])
            wide_faces[side] = both[:vectors] + both[vectors:]

    wide_faces = [None, None]

    def couplings():
        eb[0] = -jnp.concatenate(wide_faces, axis=1)
        wait_bytes(pc.at[pl.ds(0, n_row - 1)], pc_r)
        eb[2] = -lax.fori_loop(
            0, n_row, lambda i, t: t + pc[i], jnp.zeros((vectors, 2 * vectors), F32)
        )

    cuts = [n_row * i // 5 for i in range(1, 5)]

    def nothing():
        pass

    def begin():
        faces()
        plenum_start()
        plenum(0, cuts[0])

    def plenum_start():
        wait_bytes(info.at[pl.ds(0, n_row - 1)], info_r)
        wait_bytes(pa.at[pl.ds(0, n_row - 1)], pa_r)
        first = top_line + row * share
        pa[row] = zr[:, pl.ds(pl.multiple_of(first * depth, depth), share * depth)]

    def plenum(first, last):
        @pl.loop(first, last)
        def _(offset):
            s = peer(offset, row, n_row)
            own = pa[s]
            total = None
            for i in range(share):
                rows = []
                for k in range(2):
                    which = info[s, k : k + 1, :]
                    chosen = jnp.zeros((vectors, depth), F32)
                    gain = jnp.zeros((1, depth), F32)
                    for t in range(n_row):
                        block = pa[t, :, i * depth : (i + 1) * depth].astype(F32)
                        gain = jnp.where(which == t, tops[0][t, pl.ds(row * share + i, 1), :], gain)
                        chosen = jnp.where(which == t, block, chosen)
                    rows.append(chosen * (gain * tops[0][s, pl.ds(row * share + i, 1), :]))
                high, low = split(jnp.concatenate(rows, axis=0))
                mine = own[:, i * depth : (i + 1) * depth]
                part = dot_t(
                    jnp.concatenate([mine, mine], axis=1), jnp.concatenate([high, low], axis=1)
                )
                total = part if total is None else total + part
            pb[s] = total

            @pl.when(offset > 0)
            def _():
                remote(pb.at[s], pc.at[row], pc_s, pc_r, (s, col)).start()

            @pl.when(offset == 0)
            def _():
                pc[row] = pb[s]

    def finish_blocks():
        scale = 1.0 / (lines * depth)
        parts = (
            own_block * scale, eb[0, :, :vectors] * scale, eb[0, :, vectors:] * scale,
            eb[2, :, :vectors] * scale, eb[2, :, vectors:] * scale,
        )

        @pl.loop(0, n_row)
        def _(q):
            hits = (q == row, q == row - 1, q == row + 1, q == partner[0], q == partner[1])
            value = jnp.zeros((vectors, vectors), F32)
            for hit, part in zip(hits, parts):
                value = value + jnp.where(hit, 1.0, 0.0) * part
            e_ref[q] = value

    iterate, image = correct(
        1, first_side, (begin, lambda: plenum(cuts[0], cuts[1]))
    )
    defect = rhs - image
    turned = apply(3, defect, lambda: plenum(cuts[1], cuts[2]))
    shift, image = correct(
        4, project(turned), (lambda: plenum(cuts[2], cuts[3]), lambda: plenum(cuts[3], n_row))
    )
    direction, stepped = defect - shift, turned - image
    turned = apply(6, stepped, couplings)
    shift, image = correct_by_blocks(7, project(turned), (nothing, finish_blocks))
    slanted, slanted_image = stepped - shift, turned - image

    def lanes_of(left, right):
        return jnp.sum((left * right).reshape(lines, depth), axis=0, keepdims=True)

    sums = [
        lanes_of(defect, defect), lanes_of(direction, stepped), lanes_of(defect, stepped),
        lanes_of(stepped, stepped), lanes_of(slanted, stepped), lanes_of(slanted, slanted_image),
    ]
    sums = jnp.concatenate(sums + [jnp.zeros((2, depth), F32)], axis=0)
    scalar_at = lax.broadcasted_iota(jnp.int32, (8, LANES), 0) == lax.broadcasted_iota(
        jnp.int32, (8, LANES), 1
    )
    sums = jnp.where(scalar_at, jnp.sum(sums, axis=1, keepdims=True), 0.0)
    red_row[row] = jnp.sum(sums, axis=0, keepdims=True)
    for other in row_peers():
        remote(red_row.at[row], red_row.at[row], rr_s, rr_r, (other, col)).start()
    wait_bytes(red_row.at[pl.ds(0, n_row - 1)], rr_r)
    red_col[col] = jnp.sum(red_row[...], axis=0)
    ring = n_col // 2
    for i in sorted(range(1, n_col), key=lambda i: min(i % ring, ring - i % ring), reverse=True):
        remote(red_col.at[col], red_col.at[col], rc_s, rc_r, (row, peer(i, col, n_col))).start()
    wait_bytes(red_col.at[pl.ds(0, n_col - 1)], rc_r)
    scalars = jnp.where(scalar_at, jnp.sum(red_col[...], axis=0), 0.0)
    scalars = jnp.sum(scalars, axis=1, keepdims=True)
    norm, curve, cross, square, mixed, slant = [scalars[i : i + 1, :] for i in range(6)]
    alpha = norm / curve
    after = norm - 2.0 * alpha * cross + alpha * alpha * square
    gain = 1.0 + after / norm
    curve = gain * gain * curve - 2.0 * gain * alpha * mixed + alpha * alpha * slant
    last = after / curve

    def scaled(factor, values):
        return jnp.broadcast_to(factor, values.shape) * values

    alpha, gain, last = alpha[None], gain[None], last[None]
    x_ref[...] = (
        iterate
        + scaled(alpha, direction)
        + scaled(last, scaled(gain, direction) - scaled(alpha, slanted))
    )
    r_ref[...] = (
        defect
        - scaled(alpha, stepped)
        - scaled(last, scaled(gain, stepped) - scaled(alpha, slanted_image))
    )

    for at in range(ROUNDS):
        if at in COARSE_ROUNDS:
            for copy in coarse_copies(at):
                copy.wait_send()
            wait_bytes(coarse_rows[at].at[pl.ds(0, n_row - 1), pl.ds(0, 1)], top_s.at[at])
        else:
            for copy in x_copies(at) + y_copies(at):
                copy.wait_send()
            wait_bytes(tops[at].at[pl.ds(0, n_row - 1)], top_s.at[at])

    for copy in face_copies() + list(side_basis):
        copy.wait_send()
    wait_bytes(info.at[pl.ds(0, n_row - 1)], info_s)
    wait_bytes(pa.at[pl.ds(0, n_row - 1)], pa_s)
    wait_bytes(pc.at[pl.ds(0, n_row - 1)], pc_s)
    wait_bytes(red_row.at[pl.ds(0, n_row - 1)], rr_s)
    wait_bytes(red_col.at[pl.ds(0, n_col - 1)], rc_s)


def body(n_row, n_col, rhs, material, capacity, conductivity, vent, partners, basis):
    layers, width, depth = rhs.shape
    vectors = basis.shape[0]
    lines, share = layers * width, width // n_row
    smem, vmem = pl.BlockSpec(memory_space=pltpu.SMEM), pl.BlockSpec(memory_space=pltpu.VMEM)
    hbm = pl.BlockSpec(memory_space=pltpu.HBM)
    outer = 2 * (layers - 1) + width
    dma = pltpu.SemaphoreType.DMA
    scratch = [
        pltpu.VMEM(rhs.shape, F32), pltpu.VMEM(material.shape, jnp.int32),
        pltpu.VMEM(vent.shape, F32), pltpu.VMEM((vectors, lines, depth), BF16),
        pltpu.VMEM((ROUNDS, layers, width + 16, depth), F32),
        pltpu.VMEM((ROUNDS, 8, LANES), F32),
        pltpu.VMEM((ROUNDS, 2, 8, LANES), F32),
        pltpu.VMEM((n_row, 8, LANES), F32),
        pltpu.VMEM((vectors * PITCH, depth), F32),
        pltpu.VMEM((vectors * (lines + width), depth), F32),
        pltpu.VMEM((vectors, lines * depth), BF16),
        pltpu.VMEM((vectors, depth), F32),
        pltpu.VMEM((vectors, depth), BF16),
        pltpu.VMEM((2, vectors, depth), BF16),
        pltpu.VMEM((3, vectors, 2 * vectors), F32),
        pltpu.VMEM((len(COARSE_ROUNDS), 8, LANES), F32),
        pltpu.VMEM((len(COARSE_ROUNDS), 2, 8, LANES), F32),
        pltpu.VMEM((2 * vectors, lines * depth), BF16),
        pltpu.VMEM((2, vectors, layers * depth), BF16),
        pltpu.VMEM((n_row, vectors, share * depth), BF16),
        pltpu.VMEM((n_row, vectors, 2 * vectors), F32),
        pltpu.VMEM((n_row, vectors, 2 * vectors), F32),
        pltpu.VMEM((5, lines, depth), F32),
        pltpu.VMEM((vectors, (outer + 1) * depth), BF16),
        pltpu.VMEM((lines, depth), F32),
        pltpu.VMEM((vectors, depth), F32),
        pltpu.VMEM((vectors, vectors), F32),
        pltpu.VMEM((n_row, 1, LANES), F32),
        pltpu.VMEM((n_col, 1, LANES), F32),
        dma((4,)), dma((ROUNDS,)), dma((ROUNDS,)), dma((ROUNDS, 2)), dma((ROUNDS, 2)),
        dma((ROUNDS, 2)), dma((ROUNDS, 2)), dma, dma, dma((2,)), dma((2,)), dma((2, layers)), dma((2, layers)),
        dma, dma, dma, dma, dma, dma, dma, dma,
        *[pltpu.VMEM((n_row, width, depth), F32) for _ in range(ROUNDS)],
        *[pltpu.VMEM((n_row, 8, LANES), F32) for _ in COARSE_ROUNDS],
    ]
    iterate, defect, blocks = pl.pallas_call(
        functools.partial(kernel, n_row, n_col),
        out_shape=(
            jax.ShapeDtypeStruct(rhs.shape, F32),
            jax.ShapeDtypeStruct(rhs.shape, F32),
            jax.ShapeDtypeStruct((n_row, vectors, vectors), F32),
        ),
        in_specs=[smem, smem, smem, hbm, hbm, hbm, hbm],
        out_specs=(vmem, vmem, vmem),
        scratch_shapes=scratch,
        compiler_params=pltpu.CompilerParams(
            collective_id=0, has_side_effects=True, vmem_limit_bytes=48 * 1024 * 1024
        ),
        name="deflated_cg",
    )(
        *[
            pltpu.with_memory_space_constraint(array, pltpu.HBM)
            for array in (
                capacity, conductivity, partners.reshape(-1),
                rhs, material, vent, basis.reshape(vectors, lines, depth),
            )
        ],
    )
    return iterate, defect, blocks[None, None]


def solution(mesh):
    n_row, n_col = mesh.shape["row"], mesh.shape["col"]
    return jax.shard_map(
        functools.partial(body, n_row, n_col),
        mesh=mesh,
        in_specs=(
            P(None, "row", "col"),
            P(None, "row", "col"),
            P(),
            P(),
            P("row", "col"),
            P("row", "col", None),
            P(None, None, "row", "col"),
        ),
        out_specs=(P(None, "row", "col"), P(None, "row", "col"), P("row", "col", None, None, None)),
        check_vma=False,
    )
```

```python
import functools

import jax
import jax.numpy as jnp
from jax import lax
from jax.experimental import pallas as pl
from jax.experimental.pallas import tpu as pltpu
from jax.sharding import PartitionSpec as P

MESH = pl.DeviceIdType.MESH
F32, BF16 = jnp.float32, jnp.bfloat16
LANES = 128
PIVOTS = 8
ROUNDS = 9
PITCH = 72
COARSE_ROUNDS = (7,)


def harmonic(left_side, right_side):
    return 2.0 * left_side * right_side / (left_side + right_side)


def split(values):
    high = values.astype(BF16)
    return high, (values - high.astype(F32)).astype(BF16)


def dot_t(left, right):
    return lax.dot_general(left, right, (((1,), (1,)), ((), ())), preferred_element_type=F32)


def inverse(matrix):
    n = matrix.shape[0]
    row_id = lax.broadcasted_iota(jnp.int32, (n, n), 0)
    col_id = lax.broadcasted_iota(jnp.int32, (n, n), 1)
    work = jnp.concatenate([matrix, (row_id == col_id).astype(F32)], axis=1)
    wide_row = lax.broadcasted_iota(jnp.int32, work.shape, 0)
    for base in range(0, n, PIVOTS):
        ids = range(PIVOTS)
        rows = [work[base + i : base + i + 1, :] for i in ids]
        pivot = [
            [jnp.broadcast_to(rows[i][:, base + j : base + j + 1], rows[i].shape) for j in ids]
            for i in ids
        ]
        inside = (wide_row >= base) & (wide_row < base + PIVOTS)
        columns = [
            jnp.where(
                inside,
                jnp.where(wide_row == base + j, -1.0, 0.0),
                jnp.broadcast_to(work[:, base + j : base + j + 1], work.shape),
            )
            for j in ids
        ]
        work = jnp.where(inside, 0.0, work)
        for p in range(0, PIVOTS, 2):
            (a, b), (c, d) = (pivot[p + i][p : p + 2] for i in range(2))
            scale = 1.0 / (a * d - b * c)
            a, b, c, d = d * scale, -b * scale, -c * scale, a * scale
            rows[p], rows[p + 1] = a * rows[p] + b * rows[p + 1], c * rows[p] + d * rows[p + 1]
            for j in range(p + 2, PIVOTS):
                first, second = pivot[p][j], pivot[p + 1][j]
                pivot[p][j], pivot[p + 1][j] = a * first + b * second, c * first + d * second
            for i in ids:
                if i not in (p, p + 1):
                    first, second = pivot[i][p], pivot[i][p + 1]
                    rows[i] = rows[i] - (first * rows[p] + second * rows[p + 1])
                    for j in range(p + 2, PIVOTS):
                        pivot[i][j] = pivot[i][j] - (
                            first * pivot[p][j] + second * pivot[p + 1][j]
                        )
        for j in ids:
            work = work - columns[j] * rows[j]
    return work[:, n:]


def kernel(
    n_row, n_col,
    cap_ref, con_ref, par_ref, rhs_hbm, mat_hbm, vent_hbm, basis_hbm,
    x_ref, r_ref, e_ref,
    rhs_ref, mat_ref, vent_ref, basis_ref,
    fields, ysend, yrecv, info, zf, zk, zr, yb, ybs, ybr, eb, ysv, yrv, az, xb, pa, pb, pc, coef, zo, work, wide, inv_ref,
    red_row, red_col, load,
    top_s, top_r, x_s, x_r, y_s, y_r, info_s, info_r, yb_s, yb_r, xb_s, xb_r, pa_s, pa_r, pc_s, pc_r,
    rr_s, rr_r, rc_s, rc_r, *more,
):
    tops, coarse_rows = more[:ROUNDS], dict(zip(COARSE_ROUNDS, more[ROUNDS:]))
    layers, width, depth = rhs_ref.shape
    vectors = basis_ref.shape[0]
    lines = layers * width
    share = width // n_row
    row, col = lax.axis_index("row"), lax.axis_index("col")
    row_up, row_dn = lax.rem(row + 1, n_row), lax.rem(row + n_row - 1, n_row)
    col_up, col_dn = lax.rem(col + 1, n_col), lax.rem(col + n_col - 1, n_col)

    count_x = n_row // 4
    steps = [(dx, dy, dc) for dx in range(count_x) for dy in range(2) for dc in range(2)]
    steps = sorted(steps[1:], key=lambda s: (min(s[0], count_x - s[0]) + s[1], s), reverse=True)

    def peer(i, me, count):
        return lax.rem(me + i, count)

    def row_peers():
        x, rest = row // 4, lax.rem(row, 4)
        for dx, dy, dc in steps:
            yield (
                lax.rem(x + dx, count_x) * 4
                + lax.rem(rest // 2 + dy, 2) * 2
                + lax.rem(lax.rem(rest, 2) + dc, 2)
            )

    def remote(src, dst, send, recv, target):
        return pltpu.make_async_remote_copy(
            src_ref=src, dst_ref=dst, send_sem=send, recv_sem=recv,
            device_id=target, device_id_type=MESH,
        )

    def wait_bytes(ref, sem):
        pltpu.make_async_copy(ref, ref, sem).wait()

    barrier = pltpu.get_barrier_semaphore()

    @pl.loop(1, n_row)
    def _(i):
        pl.semaphore_signal(
            barrier, inc=1, device_id=(peer(i, row, n_row), col), device_id_type=MESH
        )

    for neighbour in (col_up, col_dn):
        pl.semaphore_signal(barrier, inc=1, device_id=(row, neighbour), device_id_type=MESH)

    loads = [
        pltpu.make_async_copy(src, dst, load.at[i])
        for i, (src, dst) in enumerate(
            (
                (mat_hbm, mat_ref), (vent_hbm, vent_ref),
                (rhs_hbm, rhs_ref), (basis_hbm, basis_ref),
            )
        )
    ]
    for copy in loads:
        copy.start()
    for copy in loads[:2]:
        copy.wait()

    material = mat_ref[...]
    conduct = jnp.zeros(material.shape, F32)
    heat = jnp.zeros(material.shape, F32)
    for class_id in range(con_ref.shape[0]):
        hit = material == class_id
        conduct = jnp.where(hit, con_ref[class_id], conduct)
        heat = jnp.where(hit, cap_ref[class_id], heat)
    vent = vent_ref[...]
    partner = [par_ref[k] for k in range(2)]
    info_row = lax.broadcasted_iota(jnp.int32, (8, LANES), 0)
    info[row] = jnp.where(
        info_row == 0, partner[0].astype(F32), jnp.where(info_row == 1, partner[1].astype(F32), 0.0)
    )
    line_id = lax.broadcasted_iota(jnp.int32, (lines, depth), 0)
    lane_id = lax.broadcasted_iota(jnp.int32, (lines, depth), 1)
    on_first, on_last = lane_id == line_id, lane_id == line_id + lines

    def pack_sides(first, last):
        spread = jnp.where(on_first, first, 0.0) + jnp.where(on_last, last, 0.0)
        return jnp.sum(spread, axis=0, keepdims=True)

    def send_sides(at, packed):
        ysend[at] = jnp.broadcast_to(packed, (8, LANES))
        for copy in y_copies(at):
            copy.start()

    def send_top(at, top):
        tops[at][row] = top
        for other in row_peers():
            remote(
                tops[at].at[row], tops[at].at[row], top_s.at[at], top_r.at[at], (other, col)
            ).start()

    def send_lines(at, values):
        fields[at, :, 8 : 8 + width, :] = values
        for copy in x_copies(at):
            copy.start()

    def start_exchange(at, values, top):
        flat = values.reshape(lines, depth)
        send_top(at, top)
        send_sides(at, pack_sides(flat[:, 0:1], flat[:, depth - 1 : depth]))
        send_lines(at, values)

    def x_copies(at):
        return (
            remote(
                fields.at[at, :, pl.ds(7 + width, 1), :], fields.at[at, :, pl.ds(7, 1), :],
                x_s.at[at, 0], x_r.at[at, 0], (row_up, col),
            ),
            remote(
                fields.at[at, :, pl.ds(8, 1), :], fields.at[at, :, pl.ds(8 + width, 1), :],
                x_s.at[at, 1], x_r.at[at, 1], (row_dn, col),
            ),
        )

    def y_copies(at):
        return (
            remote(ysend.at[at], yrecv.at[at, 0], y_s.at[at, 0], y_r.at[at, 0], (row, col_up)),
            remote(ysend.at[at], yrecv.at[at, 1], y_s.at[at, 1], y_r.at[at, 1], (row, col_dn)),
        )

    def finish_exchange(at, values):
        for copy in x_copies(at):
            copy.wait_recv()
        wait_bytes(tops[at].at[pl.ds(0, n_row - 1)], top_r.at[at])
        for copy in y_copies(at):
            copy.wait_recv()
        flat = values.reshape(lines, depth)
        from_dn = jnp.where(on_last, yrecv[at, 0, 0:1, :], 0.0)
        from_up = jnp.where(on_first, yrecv[at, 1, 0:1, :], 0.0)
        dn_y = jnp.where(
            lane_id == 0, jnp.sum(from_dn, axis=1, keepdims=True), pltpu.roll(flat, 1, 1)
        ).reshape(values.shape)
        up_y = jnp.where(
            lane_id == depth - 1,
            jnp.sum(from_up, axis=1, keepdims=True),
            pltpu.roll(flat, depth - 1, 1),
        ).reshape(values.shape)
        dn_x = fields[at, :, 7 : 7 + width, :]
        up_x = fields[at, :, 9 : 9 + width, :]
        coupled = tops[at][partner[0]] + tops[at][partner[1]]
        return up_x, dn_x, up_y, dn_y, coupled

    pl.semaphore_wait(barrier, n_row - 1 + 2)
    start_exchange(0, conduct, vent)

    @pl.loop(1, n_row)
    def _(i):
        remote(info.at[row], info.at[row], info_s, info_r, (peer(i, row, n_row), col)).start()

    for copy in loads[2:]:
        copy.wait()

    @pl.loop(0, vectors, unroll=4)
    def _(a):
        zf[pl.ds(a * PITCH, lines), :] = basis_ref[a].astype(F32)

    zk[lines * vectors :, :] = jnp.zeros((width * vectors, depth), F32)

    def line(k):
        return pl.ds(k * vectors, vectors)

    basis_lane = lax.broadcasted_iota(jnp.int32, (vectors, depth), 1)

    def turn(k, sides):
        block = zf[pl.ds(k, vectors, stride=PITCH), :]
        zk[line(k), :] = block
        zr[:, pl.ds(pl.multiple_of(k * depth, depth), depth)] = block.astype(BF16)
        sides = jnp.where(basis_lane == k, block[:, 0:1], sides)
        return jnp.where(basis_lane == lines + k, block[:, depth - 1 : depth], sides)

    yb[...] = lax.fori_loop(0, lines, turn, jnp.zeros((vectors, depth), F32), unroll=8)
    ybs[...] = yb[...].astype(BF16)
    side_basis = (
        remote(ybs, ybr.at[0], yb_s.at[0], yb_r.at[0], (row, col_up)),
        remote(ybs, ybr.at[1], yb_s.at[1], yb_r.at[1], (row, col_dn)),
    )

    def cells(k):
        return pl.ds(pl.multiple_of(k * depth, depth), depth)

    def face_copies():
        copies = []
        for z in range(layers):
            there = pl.ds(z * depth, depth)
            copies.append(
                remote(
                    zr.at[:, cells(z * width + width - 1)], xb.at[0, :, there],
                    xb_s.at[0, z], xb_r.at[0, z], (row_up, col),
                )
            )
            copies.append(
                remote(
                    zr.at[:, cells(z * width)], xb.at[1, :, there],
                    xb_s.at[1, z], xb_r.at[1, z], (row_dn, col),
                )
            )
        return copies

    top_line = (layers - 1) * width
    for copy in face_copies() + list(side_basis):
        copy.start()

    @pl.loop(1, n_row)
    def _(i):
        target = peer(i, row, n_row)
        first = top_line + target * share
        remote(
            zr.at[:, pl.ds(pl.multiple_of(first * depth, depth), share * depth)], pa.at[row],
            pa_s, pa_r, (target, col),
        ).start()

    def project(values):
        work[...] = values.reshape(lines, depth)

        def step(k, total):
            return total + zk[line(k), :] * work[pl.ds(k, 1), :]

        total = lax.fori_loop(0, lines, step, jnp.zeros((vectors, depth), F32), unroll=32)
        return jnp.sum(total, axis=1, keepdims=True)

    def expand(at, coarse):
        spread = jnp.broadcast_to(coarse, wide.shape)
        wide[...] = spread
        send_sides(at, jnp.sum(spread * yb[...], axis=0, keepdims=True))

        def part(first, count):
            def step(a, total):
                return total + zf[pl.ds(a * PITCH + first, count), :] * wide[pl.ds(a, 1), :]

            return lax.fori_loop(0, vectors, step, jnp.zeros((count, depth), F32), unroll=32)

        top = part(top_line, width)
        send_top(at, vent * top)
        rest = part(0, top_line)
        total = jnp.concatenate([rest, top], axis=0).reshape(layers, width, depth)
        send_lines(at, total)
        return total

    square_row = lax.broadcasted_iota(jnp.int32, (vectors, vectors), 0)
    square_col = lax.broadcasted_iota(jnp.int32, (vectors, vectors), 1)

    def solve(right_side):
        flat = jnp.sum(jnp.where(square_row == square_col, right_side, 0.0), axis=0, keepdims=True)
        return jnp.sum(inv_ref[...] * flat, axis=1, keepdims=True)

    rhs = rhs_ref[...]
    first_side = project(rhs)

    x_id = lax.broadcasted_iota(jnp.int32, conduct.shape, 1)
    y_id = lax.broadcasted_iota(jnp.int32, conduct.shape, 2)
    x_last, x_first = x_id == width - 1, x_id == 0
    y_last, y_first = y_id == depth - 1, y_id == 0
    none = jnp.zeros((1, width, depth), F32)
    up_z = jnp.concatenate([harmonic(conduct[:-1], conduct[1:]), none], axis=0)
    dn_z = jnp.concatenate([none, up_z[:-1]], axis=0)
    in_up_x = jnp.where(x_last, 0.0, harmonic(conduct, pltpu.roll(conduct, width - 1, 1)))
    in_dn_x = jnp.where(x_first, 0.0, pltpu.roll(in_up_x, 1, 1))
    in_up_y = jnp.where(y_last, 0.0, harmonic(conduct, pltpu.roll(conduct, depth - 1, 2)))
    in_dn_y = jnp.where(y_first, 0.0, pltpu.roll(in_up_y, 1, 2))
    inside = heat + up_z + dn_z + in_up_x + in_dn_x + in_up_y + in_dn_y
    for c, part in enumerate((0.5 * inside, up_z, in_up_x, in_up_y)):
        coef[c] = part.reshape(lines, depth)

    def keep(rows, where):
        high, low = split(rows)
        az[0:vectors, where] = high
        az[vectors : 2 * vectors, where] = low

    @pl.loop(0, lines, unroll=4)
    def _(k):
        own = zk[line(k), :]

        def at(c):
            return coef[c, pl.ds(k, 1), :]

        applied = at(0) * own - at(1) * zk[line(k + width), :]
        applied = applied - at(2) * zk[line(k + 1), :] - at(3) * pltpu.roll(own, depth - 1, 1)
        keep(applied, cells(k))

    half = dot_t(az[...], zr[...])
    half = half[:vectors] + half[vectors:]
    own_block = half + half.T

    near = finish_exchange(0, conduct)
    out_up_x = jnp.where(x_last & (row < n_row - 1), harmonic(conduct, near[0]), 0.0)
    out_dn_x = jnp.where(x_first & (row > 0), harmonic(conduct, near[1]), 0.0)
    out_up_y = jnp.where(y_last & (col < n_col - 1), harmonic(conduct, near[2]), 0.0)
    out_dn_y = jnp.where(y_first & (col > 0), harmonic(conduct, near[3]), 0.0)
    up_x, dn_x = in_up_x + out_up_x, in_dn_x + out_dn_x
    up_y, dn_y = in_up_y + out_up_y, in_dn_y + out_dn_y
    outside = jnp.concatenate(
        [(out_up_x + out_dn_x)[:-1], (out_up_x + out_dn_x)[-1:] + (vent * near[4])[None]], axis=0
    )
    diagonal = inside + outside + out_up_y + out_dn_y

    outer = [z * width + x for z in range(layers - 1) for x in (0, width - 1)]
    outer += list(range(top_line, lines))
    coef[4] = outside.reshape(lines, depth)
    for i, k in enumerate(outer):
        there = pl.ds(i * depth, depth)
        keep(coef[4, k : k + 1, :] * zk[line(k), :], there)
        zo[:, there] = zr[:, cells(k)]
    side_gain = pack_sides(
        out_dn_y.reshape(lines, depth)[:, 0:1], out_up_y.reshape(lines, depth)[:, depth - 1 : depth]
    )
    there = pl.ds(len(outer) * depth, depth)
    keep(side_gain * yb[...], there)
    zo[:, there] = yb[...].astype(BF16)
    size = (len(outer) + 1) * depth
    extra = dot_t(az[:, :size], zo[...])
    own_block = own_block + extra[:vectors] + extra[vectors:]
    inv_ref[...] = inverse(own_block)

    def apply_start(at, values):
        start_exchange(at, values, vent * values[layers - 1])

    def apply_finish(at, values):
        near = finish_exchange(at, values)
        none = jnp.zeros((1, width, depth), F32)
        result = diagonal * values
        result = result - up_z * jnp.concatenate([values[1:], none], axis=0)
        result = result - dn_z * jnp.concatenate([none, values[:-1]], axis=0)
        result = result - up_x * near[0] - dn_x * near[1] - up_y * near[2] - dn_y * near[3]
        return jnp.concatenate([result[:-1], (result[-1] - vent * near[4])[None]], axis=0)

    def apply(at, values, beside):
        apply_start(at, values)
        beside()
        return apply_finish(at, values)

    def apply_coarse(at, coarse, beside):
        values = expand(at, coarse)
        beside()
        return values, apply_finish(at, values)

    def correct(at, right_side, besides):
        first, first_image = apply_coarse(at, solve(right_side), besides[0])
        second, second_image = apply_coarse(
            at + 1, solve(right_side - project(first_image)), besides[1]
        )
        return first + second, first_image + second_image

    def coarse_copies(at):
        i = COARSE_ROUNDS.index(at)
        return (
            remote(ysv.at[i], yrv.at[i, 0], y_s.at[at, 0], y_r.at[at, 0], (row, col_up)),
            remote(ysv.at[i], yrv.at[i, 1], y_s.at[at, 1], y_r.at[at, 1], (row, col_dn)),
        )

    def correct_by_blocks(at, right_side, besides):
        coarse = solve(right_side)
        i, held = COARSE_ROUNDS.index(at), coarse_rows[at]
        packed = jnp.broadcast_to(pack_sides(coarse, coarse), (8, LANES))
        ysv[i] = packed
        held[row] = packed
        for copy in coarse_copies(at):
            copy.start()
        mine = held.at[row, pl.ds(0, 1)]
        for other in row_peers():
            remote(mine, mine, top_s.at[at], top_r.at[at], (other, col)).start()
        besides[0]()
        for copy in coarse_copies(at):
            copy.wait_recv()
        wait_bytes(held.at[pl.ds(0, n_row - 1), pl.ds(0, 1)], top_r.at[at])
        first_half = lax.broadcasted_iota(jnp.int32, (1, LANES), 1) < vectors
        pairs = (
            (held[row_dn, 0:1], held[row_up, 0:1]),
            (yrv[i, 0, 0:1], yrv[i, 1, 0:1]),
            (held[partner[0], 0:1], held[partner[1], 0:1]),
        )
        total = jnp.zeros((vectors, 2 * vectors), F32)
        for pair, (left, right) in enumerate(pairs):
            total = total + eb[pair] * jnp.where(first_half, left, right)
        coarse = coarse - solve(jnp.sum(total, axis=1, keepdims=True))
        return apply_coarse(at + 1, coarse, besides[1])

    def faces():
        for copy in face_copies() + list(side_basis):
            copy.wait_recv()
        halves = [pltpu.roll(ybr[side].astype(F32), depth - lines, 1) for side in range(2)]
        high, low = split(side_gain * yb[...])
        both = dot_t(
            jnp.concatenate([high, low], axis=0),
            jnp.concatenate(
                [
                    jnp.where(basis_lane < lines, halves[0], 0.0),
                    jnp.where(basis_lane < lines, 0.0, halves[1]),
                ],
                axis=0,
            ).astype(BF16),
        )
        eb[1] = -(both[:vectors] + both[vectors:])
        for side, at, coefficient in ((0, 0, dn_x), (1, width - 1, up_x)):
            terms = [
                zk[line(z * width + at), :] * coefficient[z, at : at + 1, :] for z in range(layers)
            ]
            high, low = split(jnp.concatenate(terms, axis=1))
            both = dot_t(jnp.concatenate([high, low], axis=0), xb[side])
            wide_faces[side] = both[:vectors] + both[vectors:]

    wide_faces = [None, None]

    def couplings():
        eb[0] = -jnp.concatenate(wide_faces, axis=1)
        wait_bytes(pc.at[pl.ds(0, n_row - 1)], pc_r)
        eb[2] = -lax.fori_loop(
            0, n_row, lambda i, t: t + pc[i], jnp.zeros((vectors, 2 * vectors), F32)
        )

    cuts = [n_row * i // 5 for i in range(1, 5)]

    def nothing():
        pass

    def begin():
        faces()
        plenum_start()
        plenum(0, cuts[0])

    def plenum_start():
        wait_bytes(info.at[pl.ds(0, n_row - 1)], info_r)
        wait_bytes(pa.at[pl.ds(0, n_row - 1)], pa_r)
        first = top_line + row * share
        pa[row] = zr[:, pl.ds(pl.multiple_of(first * depth, depth), share * depth)]

    def plenum(first, last):
        @pl.loop(first, last)
        def _(offset):
            s = peer(offset, row, n_row)
            own = pa[s]
            total = None
            for i in range(share):
                rows = []
                for k in range(2):
                    which = info[s, k : k + 1, :]
                    chosen = jnp.zeros((vectors, depth), F32)
                    gain = jnp.zeros((1, depth), F32)
                    for t in range(n_row):
                        block = pa[t, :, i * depth : (i + 1) * depth].astype(F32)
                        gain = jnp.where(which == t, tops[0][t, pl.ds(row * share + i, 1), :], gain)
                        chosen = jnp.where(which == t, block, chosen)
                    rows.append(chosen * (gain * tops[0][s, pl.ds(row * share + i, 1), :]))
                high, low = split(jnp.concatenate(rows, axis=0))
                mine = own[:, i * depth : (i + 1) * depth]
                part = dot_t(
                    jnp.concatenate([mine, mine], axis=1), jnp.concatenate([high, low], axis=1)
                )
                total = part if total is None else total + part
            pb[s] = total

            @pl.when(offset > 0)
            def _():
                remote(pb.at[s], pc.at[row], pc_s, pc_r, (s, col)).start()

            @pl.when(offset == 0)
            def _():
                pc[row] = pb[s]

    def finish_blocks():
        scale = 1.0 / (lines * depth)
        parts = (
            own_block * scale, eb[0, :, :vectors] * scale, eb[0, :, vectors:] * scale,
            eb[2, :, :vectors] * scale, eb[2, :, vectors:] * scale,
        )

        @pl.loop(0, n_row)
        def _(q):
            hits = (q == row, q == row - 1, q == row + 1, q == partner[0], q == partner[1])
            value = jnp.zeros((vectors, vectors), F32)
            for hit, part in zip(hits, parts):
                value = value + jnp.where(hit, 1.0, 0.0) * part
            e_ref[q] = value

    iterate, image = correct(
        1, first_side, (begin, lambda: plenum(cuts[0], cuts[1]))
    )
    defect = rhs - image
    turned = apply(3, defect, lambda: plenum(cuts[1], cuts[2]))
    shift, image = correct(
        4, project(turned), (lambda: plenum(cuts[2], cuts[3]), lambda: plenum(cuts[3], n_row))
    )
    direction, stepped = defect - shift, turned - image
    turned = apply(6, stepped, couplings)
    shift, image = correct_by_blocks(7, project(turned), (nothing, finish_blocks))
    slanted, slanted_image = stepped - shift, turned - image

    def lanes_of(left, right):
        return jnp.sum((left * right).reshape(lines, depth), axis=0, keepdims=True)

    sums = [
        lanes_of(defect, defect), lanes_of(direction, stepped), lanes_of(defect, stepped),
        lanes_of(stepped, stepped), lanes_of(slanted, stepped), lanes_of(slanted, slanted_image),
    ]
    sums = jnp.concatenate(sums + [jnp.zeros((2, depth), F32)], axis=0)
    scalar_at = lax.broadcasted_iota(jnp.int32, (8, LANES), 0) == lax.broadcasted_iota(
        jnp.int32, (8, LANES), 1
    )
    sums = jnp.where(scalar_at, jnp.sum(sums, axis=1, keepdims=True), 0.0)
    red_row[row] = jnp.sum(sums, axis=0, keepdims=True)
    for other in row_peers():
        remote(red_row.at[row], red_row.at[row], rr_s, rr_r, (other, col)).start()
    wait_bytes(red_row.at[pl.ds(0, n_row - 1)], rr_r)
    red_col[col] = jnp.sum(red_row[...], axis=0)
    ring = n_col // 2
    for i in sorted(range(1, n_col), key=lambda i: min(i % ring, ring - i % ring), reverse=True):
        remote(red_col.at[col], red_col.at[col], rc_s, rc_r, (row, peer(i, col, n_col))).start()
    wait_bytes(red_col.at[pl.ds(0, n_col - 1)], rc_r)
    scalars = jnp.where(scalar_at, jnp.sum(red_col[...], axis=0), 0.0)
    scalars = jnp.sum(scalars, axis=1, keepdims=True)
    norm, curve, cross, square, mixed, slant = [scalars[i : i + 1, :] for i in range(6)]
    alpha = norm / curve
    after = norm - 2.0 * alpha * cross + alpha * alpha * square
    gain = 1.0 + after / norm
    curve = gain * gain * curve - 2.0 * gain * alpha * mixed + alpha * alpha * slant
    last = after / curve

    def scaled(factor, values):
        return jnp.broadcast_to(factor, values.shape) * values

    alpha, gain, last = alpha[None], gain[None], last[None]
    x_ref[...] = (
        iterate
        + scaled(alpha, direction)
        + scaled(last, scaled(gain, direction) - scaled(alpha, slanted))
    )
    r_ref[...] = (
        defect
        - scaled(alpha, stepped)
        - scaled(last, scaled(gain, stepped) - scaled(alpha, slanted_image))
    )

    for at in range(ROUNDS):
        if at in COARSE_ROUNDS:
            for copy in coarse_copies(at):
                copy.wait_send()
            wait_bytes(coarse_rows[at].at[pl.ds(0, n_row - 1), pl.ds(0, 1)], top_s.at[at])
        else:
            for copy in x_copies(at) + y_copies(at):
                copy.wait_send()
            wait_bytes(tops[at].at[pl.ds(0, n_row - 1)], top_s.at[at])

    for copy in face_copies() + list(side_basis):
        copy.wait_send()
    wait_bytes(info.at[pl.ds(0, n_row - 1)], info_s)
    wait_bytes(pa.at[pl.ds(0, n_row - 1)], pa_s)
    wait_bytes(pc.at[pl.ds(0, n_row - 1)], pc_s)
    wait_bytes(red_row.at[pl.ds(0, n_row - 1)], rr_s)
    wait_bytes(red_col.at[pl.ds(0, n_col - 1)], rc_s)


def body(n_row, n_col, rhs, material, capacity, conductivity, vent, partners, basis):
    layers, width, depth = rhs.shape
    vectors = basis.shape[0]
    lines, share = layers * width, width // n_row
    smem, vmem = pl.BlockSpec(memory_space=pltpu.SMEM), pl.BlockSpec(memory_space=pltpu.VMEM)
    hbm = pl.BlockSpec(memory_space=pltpu.HBM)
    outer = 2 * (layers - 1) + width
    dma = pltpu.SemaphoreType.DMA
    scratch = [
        pltpu.VMEM(rhs.shape, F32), pltpu.VMEM(material.shape, jnp.int32),
        pltpu.VMEM(vent.shape, F32), pltpu.VMEM((vectors, lines, depth), BF16),
        pltpu.VMEM((ROUNDS, layers, width + 16, depth), F32),
        pltpu.VMEM((ROUNDS, 8, LANES), F32),
        pltpu.VMEM((ROUNDS, 2, 8, LANES), F32),
        pltpu.VMEM((n_row, 8, LANES), F32),
        pltpu.VMEM((vectors * PITCH, depth), F32),
        pltpu.VMEM((vectors * (lines + width), depth), F32),
        pltpu.VMEM((vectors, lines * depth), BF16),
        pltpu.VMEM((vectors, depth), F32),
        pltpu.VMEM((vectors, depth), BF16),
        pltpu.VMEM((2, vectors, depth), BF16),
        pltpu.VMEM((3, vectors, 2 * vectors), F32),
        pltpu.VMEM((len(COARSE_ROUNDS), 8, LANES), F32),
        pltpu.VMEM((len(COARSE_ROUNDS), 2, 8, LANES), F32),
        pltpu.VMEM((2 * vectors, lines * depth), BF16),
        pltpu.VMEM((2, vectors, layers * depth), BF16),
        pltpu.VMEM((n_row, vectors, share * depth), BF16),
        pltpu.VMEM((n_row, vectors, 2 * vectors), F32),
        pltpu.VMEM((n_row, vectors, 2 * vectors), F32),
        pltpu.VMEM((5, lines, depth), F32),
        pltpu.VMEM((vectors, (outer + 1) * depth), BF16),
        pltpu.VMEM((lines, depth), F32),
        pltpu.VMEM((vectors, depth), F32),
        pltpu.VMEM((vectors, vectors), F32),
        pltpu.VMEM((n_row, 1, LANES), F32),
        pltpu.VMEM((n_col, 1, LANES), F32),
        dma((4,)), dma((ROUNDS,)), dma((ROUNDS,)), dma((ROUNDS, 2)), dma((ROUNDS, 2)),
        dma((ROUNDS, 2)), dma((ROUNDS, 2)), dma, dma, dma((2,)), dma((2,)), dma((2, layers)), dma((2, layers)),
        dma, dma, dma, dma, dma, dma, dma, dma,
        *[pltpu.VMEM((n_row, width, depth), F32) for _ in range(ROUNDS)],
        *[pltpu.VMEM((n_row, 8, LANES), F32) for _ in COARSE_ROUNDS],
    ]
    iterate, defect, blocks = pl.pallas_call(
        functools.partial(kernel, n_row, n_col),
        out_shape=(
            jax.ShapeDtypeStruct(rhs.shape, F32),
            jax.ShapeDtypeStruct(rhs.shape, F32),
            jax.ShapeDtypeStruct((n_row, vectors, vectors), F32),
        ),
        in_specs=[smem, smem, smem, hbm, hbm, hbm, hbm],
        out_specs=(vmem, vmem, vmem),
        scratch_shapes=scratch,
        compiler_params=pltpu.CompilerParams(
            collective_id=0, has_side_effects=True, vmem_limit_bytes=48 * 1024 * 1024
        ),
        name="deflated_cg",
    )(
        *[
            pltpu.with_memory_space_constraint(array, pltpu.HBM)
            for array in (
                capacity, conductivity, partners.reshape(-1),
                rhs, material, vent, basis.reshape(vectors, lines, depth),
            )
        ],
    )
    return iterate, defect, blocks[None, None]


def solution(mesh):
    n_row, n_col = mesh.shape["row"], mesh.shape["col"]
    return jax.shard_map(
        functools.partial(body, n_row, n_col),
        mesh=mesh,
        in_specs=(
            P(None, "row", "col"),
            P(None, "row", "col"),
            P(),
            P(),
            P("row", "col"),
            P("row", "col", None),
            P(None, None, "row", "col"),
        ),
        out_specs=(P(None, "row", "col"), P(None, "row", "col"), P("row", "col", None, None, None)),
        check_vma=False,
    )
```
